128 devices in a mesh: gx: 4 (over x), gy: 4 (over z), gz: 8 (over y, core).
Axes of the slice: x: 4, y: 4, z: 4, core: 2. Of those that a mesh axis runs over, the one named last changes fastest.
Arguments:
- right_side: float32 [128, 128, 1024], P('gx', 'gy', 'gz'), may hold values from -6 to 6
- coefficient: float32 [128, 128, 1024], P('gx', 'gy', 'gz'), may hold values from 0.1 to 10
Outputs:
- solution: float32 [128, 128, 1024], P('gx', 'gy', 'gz')
The draws below stay inside these ranges and needn't reach their ends.
All inputs are finite; a program needn't handle non-finite values.
Results may differ from the reference program's by a relative error of at most 0.00002.
Values sent between devices are 32-bit elements; how exact they have to be, the bound alone decides.
A program may use at most 192 MiB of HBM per device.

```python
import math
import jax
import jax.numpy as jnp

COARSE_SWEEPS = 4
NX = 128
NY = 128
NZ = 1024


def shard_levels(rng, shape, split, smallest, top_value):
    loudness = 1.0
    for dim, shards_of in split:
        heights = jax.random.uniform(jax.random.fold_in(jax.random.fold_in(rng, 6), dim), (shards_of,), jnp.float32, smallest / len(split), top_value / len(split))
        loudness = loudness * jnp.repeat(jnp.exp(heights), shape[dim] // shards_of).reshape((-1,) + (1,) * (len(shape) - 1 - dim))
    return loudness


def normal_values(stream_key, shape, deviation, reach, pieces=(), dtype=jnp.bfloat16):
    array = jax.random.normal(stream_key, shape, jnp.float32) * deviation
    if len(pieces) > 0:
        array = shard_levels(stream_key, shape, pieces, -0.22, 0.18) * array
    return jnp.clip(array, min=-reach, max=reach).astype(dtype)


def setup_inputs(seed: int = 0) -> dict:
    keys = jax.random.split(jax.random.key(seed), 3)
    return {
        "right_side": normal_values(keys[0], (NX, NY, NZ), 1.0, 6.0, ((0, 4), (1, 4), (2, 8)), jnp.float32),
        "coefficient": jnp.clip(jnp.exp(math.log(10.0) - 4.6051702 * jax.random.uniform(keys[1], (NX, NY, NZ), jnp.float32) ** shard_levels(keys[1], (NX, NY, NZ), ((0, 4), (1, 4), (2, 8)), -0.2, 0.2)), 0.1, 10.0),
    }


def offsets_list():
    found = []
    for step_x in (-1, 0, 1):
        for step_y in (-1, 0, 1):
            for step_z in (-1, 0, 1):
                count = abs(step_x) + abs(step_y) + abs(step_z)
                if count > 0:
                    found.append((step_x, step_y, step_z, [1.0, 0.5, 0.25][count - 1]))
    return found


def shifted(padded, step_x, step_y, step_z):
    size_x, size_y, size_z = padded.shape
    return padded[1 + step_x:size_x - 1 + step_x, 1 + step_y:size_y - 1 + step_y, 1 + step_z:size_z - 1 + step_z]


def diag_region(coef_pad, scale):
    centre = shifted(coef_pad, 0, 0, 0)
    total = jnp.zeros_like(centre)
    for step_x, step_y, step_z, weight in offsets_list():
        total = total + weight * 0.5 * (centre + shifted(coef_pad, step_x, step_y, step_z))
    return scale * total


def apply_region(field_pad, coef_pad, scale):
    centre = shifted(coef_pad, 0, 0, 0)
    middle = shifted(field_pad, 0, 0, 0)
    total = jnp.zeros_like(centre)
    for step_x, step_y, step_z, weight in offsets_list():
        total = total + weight * 0.5 * (centre + shifted(coef_pad, step_x, step_y, step_z)) * (middle - shifted(field_pad, step_x, step_y, step_z))
    return scale * total


def step_sizes(sweeps):
    return [1.0 / (1.15 + 0.85 * math.cos(math.pi * (2 * j + 1) / (2 * sweeps))) for j in range(sweeps)]


def smooth(field, rhs, coef_pad, diag, scale, sweeps):
    for tau in step_sizes(sweeps):
        image = apply_region(jnp.pad(field, 1), coef_pad, scale)
        field = field + tau * (rhs - image) / diag
    return field


def restrict(field):
    size_x, size_y, size_z = field.shape
    return field.reshape(size_x // 2, 2, size_y // 2, 2, size_z // 2, 2).mean(axis=(1, 3, 5))


def prolong(field):
    size_x, size_y, size_z = field.shape
    grown = jnp.broadcast_to(field[:, None, :, None, :, None], (size_x, 2, size_y, 2, size_z, 2))
    return grown.reshape(2 * size_x, 2 * size_y, 2 * size_z)


def reference(right_side, coefficient):
    coef_one = restrict(coefficient)
    coef_two = restrict(coef_one)
    pad_zero = jnp.pad(coefficient, 1)
    pad_one = jnp.pad(coef_one, 1)
    pad_two = jnp.pad(coef_two, 1)
    diag_zero = diag_region(pad_zero, 1.0)
    diag_one = diag_region(pad_one, 0.25)
    diag_two = diag_region(pad_two, 0.0625)
    fine_u = smooth(jnp.zeros_like(right_side), right_side, pad_zero, diag_zero, 1.0, 2)
    rhs_one = restrict(right_side - apply_region(jnp.pad(fine_u, 1), pad_zero, 1.0))
    mid_u = smooth(jnp.zeros_like(rhs_one), rhs_one, pad_one, diag_one, 0.25, 2)
    rhs_two = restrict(rhs_one - apply_region(jnp.pad(mid_u, 1), pad_one, 0.25))
    coarse_u = smooth(jnp.zeros_like(rhs_two), rhs_two, pad_two, diag_two, 0.0625, COARSE_SWEEPS)
    mid_u = smooth(mid_u + prolong(coarse_u), rhs_one, pad_one, diag_one, 0.25, 2)
    return smooth(fine_u + prolong(mid_u), right_side, pad_zero, diag_zero, 1.0, 2)
```

```python
import functools
import math

import jax
import jax.numpy as jnp
from jax import lax
from jax.experimental import pallas as pl
from jax.experimental.pallas import tpu as pltpu
from jax.sharding import PartitionSpec as P

MESH = pl.DeviceIdType.MESH
F32 = jnp.float32

PX0, ROW = 4, 8
PX1 = 6
W_C0, W_F0, W_C1, W_C2, W_F1, W_F2 = 4, 3, 5, 6, 4, 5
LANE1, LANE2 = 32, 48

DIRS = [(a, b, c) for a in (-1, 0, 1) for b in (-1, 0, 1) for c in (-1, 0, 1) if (a, b, c) != (0, 0, 0)]
FLAT = [d for d in DIRS if d[2] == 0]
DEEP = [d for d in DIRS if d[2] != 0]


def step_sizes(sweeps):
    return [1.0 / (1.15 + 0.85 * math.cos(math.pi * (2 * j + 1) / (2 * sweeps))) for j in range(sweeps)]


def cut(step, low, size, width):
    if step == 0:
        return pl.ds(low, size), pl.ds(low, size)
    if step > 0:
        return pl.ds(low + size - width, width), pl.ds(low - width, width)
    return pl.ds(low, width), pl.ds(low + size, width)


def kernel(
    shape, right_hbm, coef_hbm, out_ref,
    c0, f0, k0, q0, ua, wa, ub, wb,
    oc, ocl, ocr, of, ofl, ofr,
    sc, sf, sk, sq, sua, swa, sub, swb, yc, yu, yw, sp,
    t0, p0s, t1, p1s,
    c1, c1l, c1r, f1, f1l, f1r, cm1, fm1, k1, q1, ua1, wa1, ub1, wb1,
    c2, c2l, c2r, f2, f2l, f2r, cm2, fm2, k2, q2, ua2, wa2, ub2, wb2,
    in_sem, send_sem, recv_sem,
):
    spot = [lax.axis_index(a) for a in ("gx", "gy", "gz")]
    below = [s > 0 for s in spot]
    above = [s < n - 1 for s, n in zip(spot, shape)]

    def exists(d):
        found = None
        for axis, step in enumerate(d):
            if step != 0:
                one = above[axis] if step > 0 else below[axis]
                found = one if found is None else jnp.logical_and(found, one)
        return found

    def opposite(d):
        return tuple(-s for s in d)

    def device(d):
        return tuple(s + step for s, step in zip(spot, d))

    lane = lax.broadcasted_iota(jnp.int32, (8, 128), 1)
    group = lane & 15
    tau2 = step_sizes(2)
    tau4 = step_sizes(4)

    def roll(value, shift):
        return pltpu.roll(value, shift, axis=1)

    def pick(value, index):
        return jnp.take_along_axis(value, index, axis=1, mode="promise_in_bounds")

    def rows(ref, plane, start):
        return ref[plane, pl.ds(start, 8), :]

    in_c = pltpu.make_async_copy(coef_hbm, c0.at[pl.ds(PX0, 32), pl.ds(ROW, 32)], in_sem.at[0])
    in_f = pltpu.make_async_copy(right_hbm, f0.at[pl.ds(PX0, 32), pl.ds(ROW, 32)], in_sem.at[1])
    in_c.start()
    in_f.start()

    zero = jnp.zeros((8, 128), F32)
    for ref in (c0, f0):
        for plane in list(range(PX0)) + list(range(PX0 + 32, PX0 + 36)):
            for start in range(0, 48, 8):
                ref[plane, pl.ds(start, 8), :] = zero

    @pl.loop(0, 32)
    def _(i):
        for ref in (c0, f0):
            ref[PX0 + i, pl.ds(0, 8), :] = zero
            ref[PX0 + i, pl.ds(40, 8), :] = zero

    @pl.loop(0, 6)
    def _(i):
        for ref in (ocl, ocr, ofl, ofr):
            for start in range(0, 48, 8):
                ref[i, pl.ds(start, 8), :] = zero

    @pl.loop(0, 28)
    def _(i):
        for ref in (c1, c1l, c1r, f1, f1l, f1r):
            for start in range(0, 32, 8):
                ref[i, pl.ds(start, 8), :] = zero

    @pl.loop(0, 20)
    def _(i):
        for ref in (c2, c2l, c2r, f2, f2l, f2r):
            for start in range(0, 32, 8):
                ref[i, pl.ds(start, 8), :] = zero

    barrier = pltpu.get_barrier_semaphore()
    for d in DIRS:
        @pl.when(exists(d))
        def _():
            pl.semaphore_signal(barrier, inc=1, device_id=device(d), device_id_type=MESH)

    counter = [0]

    def message(d, src, dst):
        slot = counter[0]
        counter[0] += 1
        return pltpu.make_async_remote_copy(
            src_ref=src, dst_ref=dst, send_sem=send_sem.at[slot], recv_sem=recv_sem.at[slot],
            device_id=device(d), device_id_type=MESH,
        )

    def block_messages(own, left, right, low, size_x, size_y, width):
        found = {}
        for d in DIRS:
            from_x, to_x = cut(d[0], low, size_x, width)
            from_y, to_y = cut(d[1], ROW, size_y, width)
            target = {0: own, 1: left, -1: right}[d[2]]
            found[d] = [message(d, own.at[from_x, from_y], target.at[to_x, to_y])]
        return found

    def flat_messages(own, width):
        found = {}
        for d in FLAT:
            from_x, to_x = cut(d[0], PX0, 32, width)
            from_y, to_y = cut(d[1], ROW, 32, width)
            found[d] = [message(d, own.at[from_x, from_y], own.at[to_x, to_y])]
        return found

    def slab_messages(own, left, right, width):
        found = {}
        for d in DEEP:
            from_x, to_x = cut(d[0], 1, 4, 1)
            from_y, to_y = cut(d[1], ROW, 32, width)
            target = left if d[2] > 0 else right
            found[d] = [message(d, own.at[from_x, from_y], target.at[to_x, to_y])]
        return found

    msg_c = {**flat_messages(c0, W_C0), **slab_messages(oc, ocl, ocr, W_C0)}
    msg_f = {**flat_messages(f0, W_F0), **slab_messages(of, ofl, ofr, W_F0)}
    msg_c1 = block_messages(c1, c1l, c1r, PX1, 16, 16, W_C1)
    msg_c2 = block_messages(c2, c2l, c2r, PX1, 8, 8, W_C2)
    msg_f1 = block_messages(f1, f1l, f1r, PX1, 16, 16, W_F1)
    msg_f2 = block_messages(f2, f2l, f2r, PX1, 8, 8, W_F2)

    far_first = sorted(DIRS, key=lambda d: -sum(abs(s) for s in d))

    def start(*groups):
        for d in far_first:
            @pl.when(exists(d))
            def _():
                for found in groups:
                    for copy in found[d]:
                        copy.start()

    def arrive(*groups):
        for d in DIRS:
            @pl.when(exists(opposite(d)))
            def _():
                for found in groups:
                    for copy in found[d]:
                        copy.wait_recv()

    def sent(*groups):
        for d in DIRS:
            @pl.when(exists(d))
            def _():
                for found in groups:
                    for copy in found[d]:
                        copy.wait_send()

    def packed(ref, first, ks, start_row):
        total = jnp.zeros((8, 128), F32)
        for k in ks:
            value = rows(ref, first + k, start_row)
            low = roll(value, 16 * k + 4)
            high = roll(value, (16 * k + 12) % 128)
            total = jnp.where((lane >> 2) == 4 * k + 1, low, total)
            total = jnp.where((lane >> 2) == 4 * k + 2, high, total)
        return total

    def pack_own(ref, slab):
        @pl.loop(0, 4)
        def _(g):
            for b in range(4):
                slab[1 + g, pl.ds(ROW + 8 * b, 8), :] = packed(ref, PX0 + 8 * g, range(8), ROW + 8 * b)

    in_c.wait()
    pack_own(c0, oc)
    in_f.wait()
    pack_own(f0, of)
    pl.semaphore_wait(
        barrier,
        math.prod(1 + b.astype(jnp.int32) + a.astype(jnp.int32) for b, a in zip(below, above)) - 1,
    )
    start(msg_c)
    start(msg_f)

    def halved(value):
        return value + roll(value, 127)

    down1 = jnp.clip(2 * (lane - LANE1), 0, 127)
    own1 = jnp.logical_and(lane >= LANE1, lane < LANE1 + 64)
    down2 = jnp.clip(LANE1 + 2 * (lane - LANE2), 0, 127)
    own2 = jnp.logical_and(lane >= LANE2, lane < LANE2 + 32)

    @pl.loop(0, 16)
    def _(i):
        for b in range(2):
            total = None
            for dx in range(2):
                for dy in range(2):
                    part = c0[PX0 + 2 * i + dx, pl.ds(ROW + 16 * b + dy, 8, stride=2), :]
                    total = part if total is None else total + part
            c1[PX1 + i, pl.ds(ROW + 8 * b, 8), :] = jnp.where(own1, 0.125 * pick(halved(total), down1), 0.0)

    @pl.loop(0, 8)
    def _(i):
        total = None
        for dx in range(2):
            for dy in range(2):
                part = c1[PX1 + 2 * i + dx, pl.ds(ROW + dy, 8, stride=2), :]
                total = part if total is None else total + part
        c2[PX1 + i, pl.ds(ROW, 8), :] = jnp.where(own2, 0.125 * pick(halved(total), down2), 0.0)

    start(msg_c1, msg_c2)

    def ysum(ref, plane, start_row):
        above_, here, below_ = (rows(ref, plane, start_row + s) for s in (-1, 0, 1))
        return (above_ + below_) + (here + here)

    def zsum(value):
        return (roll(value, 1) + roll(value, 127)) + (value + value)

    def plain(refs):
        def line(i, plane, start_row):
            return zsum(ysum(refs[i], plane, start_row))

        return line

    first_lane, last_lane = lane == 0, lane == 127

    def edged(refs, edges):
        def line(i, plane, start_row):
            value = ysum(refs[i], plane, start_row)
            g = (plane + 4) >> 3
            k = (plane + 4) & 7
            edge = rows(edges[i], g, start_row)
            left = jnp.where(first_lane, roll(edge, (125 - 16 * k) & 127), roll(value, 1))
            right = jnp.where(last_lane, roll(edge, (115 - 16 * k) & 127), roll(value, 127))
            return (left + right) + (value + value)

        return line

    def sweep_planes(line, count, first_row, blocks, first, last, emit, unroll=2):
        starts = [first_row + 8 * b for b in range(blocks)]
        each = [(i, r) for i in range(count) for r in starts]
        before = [line(i, first - 1, r) for i, r in each]
        current = [line(i, first, r) for i, r in each]
        pair = [a + b for a, b in zip(before, current)]

        def body(index, carry):
            pair, current = carry
            for u in range(unroll):
                plane = first + unroll * index + u
                following = [line(i, plane + 1, r) for i, r in each]
                later = [a + b for a, b in zip(current, following)]
                sums = [a + b for a, b in zip(pair, later)]
                for b, r in enumerate(starts):
                    emit(u, index, plane, r, [sums[i * blocks + b] for i in range(count)])
                pair, current = later, following
            return tuple(pair), tuple(current)

        lax.fori_loop(0, (last - first) // unroll, body, (tuple(pair), tuple(current)))

    def slab_pass(edges, emit):
        for b in range(5):
            r = 4 + 8 * b
            sums = []
            for ref in edges:
                parts = [zsum(rows(ref, g, r)) for g in range(6)]
                up = [roll(p, 16) for p in parts]
                down = [roll(p, 112) for p in parts]
                sums.append([
                    (jnp.where(lane < 16, up[max(g - 1, 0)], up[g])
                     + jnp.where(lane >= 112, down[min(g + 1, 5)], down[g]))
                    + (parts[g] + parts[g])
                    for g in range(6)
                ])
            for g in range(6):
                emit(g, r, [s[g] for s in sums])

    def slab_ysum(ref, result):
        for g in range(6):
            for b in range(5):
                result[g, pl.ds(4 + 8 * b, 8), :] = ysum(ref, g, 4 + 8 * b)

    def first_emit(c, f, k, q, u, w, scale):
        def emit(_, __, plane, r, sums):
            at = (plane, pl.ds(r, 8), slice(None))
            centre = c[at]
            k[at] = 64.0 * centre + sums[0]
            factor = jnp.where(centre > 0.0, 1.0 / (48.0 * centre + sums[0]), 0.0)
            q[at] = factor
            if f is not None:
                value = (scale * factor) * f[at]
                u[at] = value
                w[at] = centre * value

        return emit

    def image_at(at, c, k, u, sums):
        return u[at] * k[at] - (c[at] * sums[0] + sums[1])

    def sweep_emit(c, f, k, q, u, tau, f_scale, u_out, w_out):
        def emit(_, __, plane, r, sums):
            at = (plane, pl.ds(r, 8), slice(None))
            rhs = f[at] if f_scale == 1.0 else f_scale * f[at]
            value = u[at] + (tau * q[at]) * (rhs - image_at(at, c, k, u, sums))
            u_out[at] = value
            if w_out is not None:
                w_out[at] = c[at] * value

        return emit

    def residual_emit(c, f, k, u, f_scale, low_row, result):
        held = {}

        def emit(step, index, plane, r, sums):
            at = (plane, pl.ds(r, 8), slice(None))
            rhs = f[at] if f_scale == 1.0 else f_scale * f[at]
            value = rhs - image_at(at, c, k, u, sums)
            if step == 0:
                held[r] = value
            else:
                result[index, pl.ds(r - low_row, 8), :] = halved(held[r] + value)

        return emit

    def slabbed(emit):
        return lambda g, r, sums: emit(0, 0, g, r, sums)

    arrive(msg_c, msg_f)

    def build_slab(ref, left, right, slab):
        def put(g, first, ks):
            for b in range(5):
                r = 4 + 8 * b
                middle = packed(ref, first, ks, r)
                slab[g, pl.ds(r, 8), :] = jnp.where(
                    group < 4, roll(rows(left, g, r), 120),
                    jnp.where(group < 12, middle, roll(rows(right, g, r), 8)),
                )

        put(0, -4, range(4, 8))

        @pl.loop(1, 5)
        def _(g):
            put(g, 8 * g - 4, range(8))

        put(5, 36, range(4))

    build_slab(c0, ocl, ocr, sc)
    build_slab(f0, ofl, ofr, sf)
    slab_ysum(sc, yc)
    slab_pass([yc], slabbed(first_emit(sc, sf, sk, sq, sua, swa, 8.0 * tau2[0])))
    slab_ysum(sua, yu)
    slab_ysum(swa, yw)
    sweep_planes(edged([c0], [yc]), 1, 4, 5, 1, 39, first_emit(c0, f0, k0, q0, ua, wa, 8.0 * tau2[0]))
    sweep_planes(edged([ua, wa], [yu, yw]), 2, 4, 5, 2, 38, sweep_emit(c0, f0, k0, q0, ua, tau2[1], 8.0, ub, wb))
    slab_pass([yu, yw], slabbed(sweep_emit(sc, sf, sk, sq, sua, tau2[1], 8.0, sub, swb)))
    slab_ysum(sub, yu)
    slab_ysum(swb, yw)
    sweep_planes(edged([ub, wb], [yu, yw]), 2, ROW, 4, 4, 36, residual_emit(c0, f0, k0, ub, 8.0, ROW, t0))

    @pl.loop(0, 16)
    def _(i):
        for b in range(2):
            total = t0[i, pl.ds(16 * b, 8, stride=2), :] + t0[i, pl.ds(16 * b + 1, 8, stride=2), :]
            f1[PX1 + i, pl.ds(ROW + 8 * b, 8), :] = jnp.where(own1, 0.5 * pick(total, down1), 0.0)

    start(msg_f1)

    def merge(own, left, right, result, planes, low, width):
        @pl.loop(0, planes)
        def _(i):
            for r in range(0, 32, 8):
                result[i, pl.ds(r, 8), :] = jnp.where(
                    lane < low, roll(rows(left, i, r), 128 - width),
                    jnp.where(lane < low + width, rows(own, i, r), roll(rows(right, i, r), width)),
                )

    arrive(msg_c1, msg_c2)
    merge(c1, c1l, c1r, cm1, 28, LANE1, 64)
    merge(c2, c2l, c2r, cm2, 20, LANE2, 32)
    sweep_planes(plain([cm1]), 1, 4, 3, 2, 26, first_emit(cm1, None, k1, q1, None, None, None))
    sweep_planes(plain([cm2]), 1, 3, 3, 1, 19, first_emit(cm2, None, k2, q2, None, None, None))

    def first_sweep(c, f, q, u, w, tau, first_row, blocks, first, last):
        @pl.loop(first, last)
        def _(plane):
            for b in range(blocks):
                at = (plane, pl.ds(first_row + 8 * b, 8), slice(None))
                value = (tau * q[at]) * f[at]
                u[at] = value
                w[at] = c[at] * value

    arrive(msg_f1)
    merge(f1, f1l, f1r, fm1, 28, LANE1, 64)
    first_sweep(cm1, fm1, q1, ua1, wa1, tau2[0], 4, 3, 2, 26)
    sweep_planes(plain([ua1, wa1]), 2, 4, 3, 3, 25, sweep_emit(cm1, fm1, k1, q1, ua1, tau2[1], 1.0, ub1, wb1))
    sweep_planes(plain([ub1, wb1]), 2, ROW, 2, 6, 22, residual_emit(cm1, fm1, k1, ub1, 1.0, ROW, t1))

    @pl.loop(0, 8)
    def _(i):
        total = t1[i, pl.ds(0, 8, stride=2), :] + t1[i, pl.ds(1, 8, stride=2), :]
        f2[PX1 + i, pl.ds(ROW, 8), :] = jnp.where(own2, 0.5 * pick(total, down2), 0.0)

    start(msg_f2)

    arrive(msg_f2)
    merge(f2, f2l, f2r, fm2, 20, LANE2, 32)
    first_sweep(cm2, fm2, q2, ua2, wa2, tau4[0], 3, 3, 1, 19)
    sweep_planes(plain([ua2, wa2]), 2, 4, 2, 2, 18, sweep_emit(cm2, fm2, k2, q2, ua2, tau4[1], 1.0, ub2, wb2))
    sweep_planes(plain([ub2, wb2]), 2, 4, 2, 3, 17, sweep_emit(cm2, fm2, k2, q2, ub2, tau4[2], 1.0, ua2, wa2))
    sweep_planes(plain([ua2, wa2]), 2, 4, 2, 4, 16, sweep_emit(cm2, fm2, k2, q2, ua2, tau4[3], 1.0, ub2, None))

    up = 32 + (lane >> 1)

    @pl.loop(0, 12)
    def _(i):
        for b in range(2):
            value = pick(rows(ub2, 4 + i, 6 + 8 * b), up)
            p1s[i, pl.ds(16 * b, 8, stride=2), :] = value
            p1s[i, pl.ds(16 * b + 1, 8, stride=2), :] = value

    @pl.loop(0, 12)
    def _(i):
        for dx in range(2):
            for b in range(3):
                at = (2 + 2 * i + dx, pl.ds(4 + 8 * b, 8), slice(None))
                value = ub1[at] + p1s[i, pl.ds(8 * b, 8), :]
                ua1[at] = value
                wa1[at] = cm1[at] * value

    sweep_planes(plain([ua1, wa1]), 2, 4, 3, 4, 24, sweep_emit(cm1, fm1, k1, q1, ua1, tau2[0], 1.0, ub1, wb1))
    sweep_planes(plain([ub1, wb1]), 2, 4, 3, 5, 23, sweep_emit(cm1, fm1, k1, q1, ub1, tau2[1], 1.0, ua1, None))

    side = 32 + ((group - 4 + jnp.where(group >= 8, 120, 0)) >> 1)

    @pl.loop(0, 18)
    def _(i):
        for b in range(3):
            value = pick(rows(ua1, 5 + i, 6 + 8 * b), up)
            p0s[i, pl.ds(16 * b, 8, stride=2), :] = value
            p0s[i, pl.ds(16 * b + 1, 8, stride=2), :] = value

    @pl.loop(0, 18)
    def _(i):
        for dx in range(2):
            for b in range(5):
                at = (2 + 2 * i + dx, pl.ds(4 + 8 * b, 8), slice(None))
                value = ub[at] + p0s[i, pl.ds(8 * b, 8), :]
                ua[at] = value
                wa[at] = c0[at] * value

    @pl.loop(0, 6)
    def _(g):
        for b in range(3):
            total = jnp.zeros((8, 128), F32)
            for m in range(4):
                total = jnp.where((lane >> 5) == m, pick(rows(ua1, 4 * g + 2 + m, 6 + 8 * b), side), total)
            sp[g, pl.ds(16 * b, 8, stride=2), :] = total
            sp[g, pl.ds(16 * b + 1, 8, stride=2), :] = total
        for b in range(5):
            at = (g, pl.ds(4 + 8 * b, 8), slice(None))
            value = sub[at] + sp[g, pl.ds(8 * b, 8), :]
            sua[at] = value
            swa[at] = sc[at] * value

    slab_ysum(sua, yu)
    slab_ysum(swa, yw)
    sweep_planes(edged([ua, wa], [yu, yw]), 2, 4, 5, 3, 37, sweep_emit(c0, f0, k0, q0, ua, tau2[0], 8.0, ub, wb))
    slab_pass([yu, yw], slabbed(sweep_emit(sc, sf, sk, sq, sua, tau2[0], 8.0, sub, swb)))
    slab_ysum(sub, yu)
    slab_ysum(swb, yw)

    def last_emit(_, __, plane, r, sums):
        at = (plane, pl.ds(r, 8), slice(None))
        value = ub[at] + (tau2[1] * q0[at]) * (8.0 * f0[at] - image_at(at, c0, k0, ub, sums))
        out_ref[plane - PX0, pl.ds(r - ROW, 8), :] = value

    sweep_planes(edged([ub, wb], [yu, yw]), 2, ROW, 4, 4, 36, last_emit)

    sent(msg_c, msg_f, msg_c1, msg_c2, msg_f1, msg_f2)


def solution(mesh):
    shape = tuple(mesh.shape[a] for a in ("gx", "gy", "gz"))
    count = 26 * 6
    big = [pltpu.VMEM((40, 48, 128), F32)] * 8
    slabs = [pltpu.VMEM((6, 48, 128), F32)] * 18
    level1 = [pltpu.VMEM((28, 32, 128), F32)] * 14
    level2 = [pltpu.VMEM((20, 32, 128), F32)] * 14
    between = [
        pltpu.VMEM((16, 32, 128), F32), pltpu.VMEM((18, 48, 128), F32),
        pltpu.VMEM((8, 16, 128), F32), pltpu.VMEM((12, 32, 128), F32),
    ]

    def per_device(right_side, coefficient):
        return pl.pallas_call(
            functools.partial(kernel, shape),
            out_shape=jax.ShapeDtypeStruct(right_side.shape, F32),
            in_specs=[pl.BlockSpec(memory_space=pl.ANY)] * 2,
            out_specs=pl.BlockSpec(memory_space=pltpu.VMEM),
            scratch_shapes=big + slabs + between + level1 + level2 + [
                pltpu.SemaphoreType.DMA((2,)),
                pltpu.SemaphoreType.DMA((count,)),
                pltpu.SemaphoreType.DMA((count,)),
            ],
            compiler_params=pltpu.CompilerParams(collective_id=0, has_side_effects=True),
        )(right_side, coefficient)

    placed = P("gx", "gy", "gz")
    return jax.shard_map(per_device, mesh=mesh, in_specs=(placed, placed), out_specs=placed, check_vma=False)
```

```python
import functools
import math

import jax
import jax.numpy as jnp
from jax import lax
from jax.experimental import pallas as pl
from jax.experimental.pallas import tpu as pltpu
from jax.sharding import PartitionSpec as P

MESH = pl.DeviceIdType.MESH
F32 = jnp.float32

PX0, ROW = 4, 8
PX1 = 6
W_C0, W_F0, W_C1, W_C2, W_F1, W_F2 = 4, 3, 5, 6, 4, 5
LANE1, LANE2 = 32, 48

DIRS = [(a, b, c) for a in (-1, 0, 1) for b in (-1, 0, 1) for c in (-1, 0, 1) if (a, b, c) != (0, 0, 0)]
FLAT = [d for d in DIRS if d[2] == 0]
DEEP = [d for d in DIRS if d[2] != 0]


def step_sizes(sweeps):
    return [1.0 / (1.15 + 0.85 * math.cos(math.pi * (2 * j + 1) / (2 * sweeps))) for j in range(sweeps)]


def cut(step, low, size, width):
    if step == 0:
        return pl.ds(low, size), pl.ds(low, size)
    if step > 0:
        return pl.ds(low + size - width, width), pl.ds(low - width, width)
    return pl.ds(low, width), pl.ds(low + size, width)


def kernel(
    shape, right_hbm, coef_hbm, out_ref,
    c0, f0, k0, q0, ua, wa, ub, wb,
    oc, ocl, ocr, of, ofl, ofr,
    sc, sf, sk, sq, sua, swa, sub, swb, yc, yu, yw, sp,
    t0, p0s, t1, p1s,
    c1, f1, cm1, fm1, k1, q1, ua1, wa1, ub1, wb1,
    oc1, ocl1, ocr1, of1, ofl1, ofr1,
    c2, f2, cm2, fm2, k2, q2, ua2, wa2, ub2, wb2,
    oc2, ocl2, ocr2, of2, ofl2, ofr2,
    in_sem, send_sem, recv_sem,
):
    spot = [lax.axis_index(a) for a in ("gx", "gy", "gz")]
    below = [s > 0 for s in spot]
    above = [s < n - 1 for s, n in zip(spot, shape)]

    def exists(d):
        found = None
        for axis, step in enumerate(d):
            if step != 0:
                one = above[axis] if step > 0 else below[axis]
                found = one if found is None else jnp.logical_and(found, one)
        return found

    def opposite(d):
        return tuple(-s for s in d)

    def device(d):
        return tuple(s + step for s, step in zip(spot, d))

    lane = lax.broadcasted_iota(jnp.int32, (8, 128), 1)
    group = lane & 15
    tau2 = step_sizes(2)
    tau4 = step_sizes(4)

    def roll(value, shift):
        return pltpu.roll(value, shift, axis=1)

    def pick(value, index):
        return jnp.take_along_axis(value, index, axis=1, mode="promise_in_bounds")

    def rows(ref, plane, start):
        return ref[plane, pl.ds(start, 8), :]

    in_c = pltpu.make_async_copy(coef_hbm, c0.at[pl.ds(PX0, 32), pl.ds(ROW, 32)], in_sem.at[0])
    in_f = pltpu.make_async_copy(right_hbm, f0.at[pl.ds(PX0, 32), pl.ds(ROW, 32)], in_sem.at[1])
    in_c.start()
    in_f.start()

    barrier = pltpu.get_barrier_semaphore()
    for d in DIRS:
        @pl.when(exists(d))
        def _():
            pl.semaphore_signal(barrier, inc=1, device_id=device(d), device_id_type=MESH)

    zero = jnp.zeros((8, 128), F32)
    flat = [(c0, PX0, 32, 32), (f0, PX0, 32, 32), (c1, PX1, 16, 16), (f1, PX1, 16, 16), (c2, PX1, 8, 8), (f2, PX1, 8, 8)]
    lefts = [(ocl, 1, 4, 32), (ofl, 1, 4, 32), (ocl1, 1, 2, 16), (ofl1, 1, 2, 16), (ocl2, 1, 1, 8), (ofl2, 1, 1, 8)]
    rights = [(ocr, 1, 4, 32), (ofr, 1, 4, 32), (ocr1, 1, 2, 16), (ofr1, 1, 2, 16), (ocr2, 1, 1, 8), (ofr2, 1, 1, 8)]

    def clear(ref, first, last, starts):
        @pl.loop(first, last)
        def _(i):
            for r in starts:
                ref[i, pl.ds(r, 8), :] = zero

    for axis in range(3):
        for side, present in ((0, below[axis]), (1, above[axis])):
            @pl.when(jnp.logical_not(present))
            def _():
                if axis == 2:
                    for ref, low, size_x, size_y in (lefts, rights)[side]:
                        clear(ref, 0, 2 * low + size_x, range(0, size_y + 16, 8))
                else:
                    for ref, low, size_x, size_y in flat + lefts + rights:
                        if axis == 0:
                            first = (0, low + size_x)[side]
                            clear(ref, first, first + low, range(0, size_y + 16, 8))
                        else:
                            clear(ref, 0, 2 * low + size_x, [(0, 8 + size_y)[side]])

    counter = [0]

    def message(d, src, dst):
        slot = counter[0]
        counter[0] += 1
        return pltpu.make_async_remote_copy(
            src_ref=src, dst_ref=dst, send_sem=send_sem.at[slot], recv_sem=recv_sem.at[slot],
            device_id=device(d), device_id_type=MESH,
        )

    def flat_messages(own, low, size, width):
        found = {}
        for d in FLAT:
            from_x, to_x = cut(d[0], low, size, width)
            from_y, to_y = cut(d[1], ROW, size, width)
            found[d] = [message(d, own.at[from_x, from_y], own.at[to_x, to_y])]
        return found

    def slab_messages(own, left, right, size, width):
        found = {}
        for d in DEEP:
            from_x, to_x = cut(d[0], 1, size // 8, 1)
            from_y, to_y = cut(d[1], ROW, size, width)
            target = left if d[2] > 0 else right
            found[d] = [message(d, own.at[from_x, from_y], target.at[to_x, to_y])]
        return found

    def messages(own, low, slab, left, right, size, width):
        return {**flat_messages(own, low, size, width), **slab_messages(slab, left, right, size, width)}

    msg_c = messages(c0, PX0, oc, ocl, ocr, 32, W_C0)
    msg_f = messages(f0, PX0, of, ofl, ofr, 32, W_F0)
    msg_c1 = messages(c1, PX1, oc1, ocl1, ocr1, 16, W_C1)
    msg_c2 = messages(c2, PX1, oc2, ocl2, ocr2, 8, W_C2)
    msg_f1 = messages(f1, PX1, of1, ofl1, ofr1, 16, W_F1)
    msg_f2 = messages(f2, PX1, of2, ofl2, ofr2, 8, W_F2)

    far_first = sorted(DIRS, key=lambda d: -sum(abs(s) for s in d))

    def start(*groups):
        for d in far_first:
            @pl.when(exists(d))
            def _():
                for found in groups:
                    for copy in found[d]:
                        copy.start()

    def arrive(*groups):
        for d in DIRS:
            @pl.when(exists(opposite(d)))
            def _():
                for found in groups:
                    for copy in found[d]:
                        copy.wait_recv()

    def sent(*groups):
        for d in DIRS:
            @pl.when(exists(d))
            def _():
                for found in groups:
                    for copy in found[d]:
                        copy.wait_send()

    def packed(ref, first, ks, start_row):
        total = jnp.zeros((8, 128), F32)
        for k in ks:
            value = rows(ref, first + k, start_row)
            low = roll(value, 16 * k + 4)
            high = roll(value, (16 * k + 12) % 128)
            total = jnp.where((lane >> 2) == 4 * k + 1, low, total)
            total = jnp.where((lane >> 2) == 4 * k + 2, high, total)
        return total

    def pack_own(ref, slab):
        @pl.loop(0, 4)
        def _(g):
            for b in range(4):
                slab[1 + g, pl.ds(ROW + 8 * b, 8), :] = packed(ref, PX0 + 8 * g, range(8), ROW + 8 * b)

    def pack_coarse(ref, slab, size, low):
        width = size * 4
        for g in range(size // 8):
            for b in range(size // 8):
                total = jnp.zeros((8, 128), F32)
                for k in range(8):
                    value = rows(ref, PX1 + 8 * g + k, ROW + 8 * b)
                    total = jnp.where((lane >> 3) == 2 * k, roll(value, (16 * k - low) % 128), total)
                    total = jnp.where((lane >> 3) == 2 * k + 1, roll(value, (16 * k + 16 - low - width) % 128), total)
                slab[1 + g, pl.ds(ROW + 8 * b, 8), :] = total

    in_c.wait()
    pack_own(c0, oc)
    in_f.wait()
    pack_own(f0, of)
    pl.semaphore_wait(
        barrier,
        math.prod(1 + b.astype(jnp.int32) + a.astype(jnp.int32) for b, a in zip(below, above)) - 1,
    )
    start(msg_c)
    start(msg_f)

    def halved(value):
        return value + roll(value, 127)

    down1 = jnp.clip(2 * (lane - LANE1), 0, 127)
    own1 = jnp.logical_and(lane >= LANE1, lane < LANE1 + 64)
    down2 = jnp.clip(LANE1 + 2 * (lane - LANE2), 0, 127)
    own2 = jnp.logical_and(lane >= LANE2, lane < LANE2 + 32)

    @pl.loop(0, 16)
    def _(i):
        for b in range(2):
            total = None
            for dx in range(2):
                for dy in range(2):
                    part = c0[PX0 + 2 * i + dx, pl.ds(ROW + 16 * b + dy, 8, stride=2), :]
                    total = part if total is None else total + part
            c1[PX1 + i, pl.ds(ROW + 8 * b, 8), :] = jnp.where(own1, 0.125 * pick(halved(total), down1), 0.0)

    @pl.loop(0, 8)
    def _(i):
        total = None
        for dx in range(2):
            for dy in range(2):
                part = c1[PX1 + 2 * i + dx, pl.ds(ROW + dy, 8, stride=2), :]
                total = part if total is None else total + part
        c2[PX1 + i, pl.ds(ROW, 8), :] = jnp.where(own2, 0.125 * pick(halved(total), down2), 0.0)

    pack_coarse(c1, oc1, 16, LANE1)
    pack_coarse(c2, oc2, 8, LANE2)
    start(msg_c1, msg_c2)

    def ysum(ref, plane, start_row):
        above_, here, below_ = (rows(ref, plane, start_row + s) for s in (-1, 0, 1))
        return (above_ + below_) + (here + here)

    def zsum(value):
        return (roll(value, 1) + roll(value, 127)) + (value + value)

    def plain(refs):
        def line(i, plane, start_row):
            return zsum(ysum(refs[i], plane, start_row))

        return line

    first_lane, last_lane = lane == 0, lane == 127

    def edged(refs, edges):
        def line(i, plane, start_row):
            value = ysum(refs[i], plane, start_row)
            g = (plane + 4) >> 3
            k = (plane + 4) & 7
            edge = rows(edges[i], g, start_row)
            left = jnp.where(first_lane, roll(edge, (125 - 16 * k) & 127), roll(value, 1))
            right = jnp.where(last_lane, roll(edge, (115 - 16 * k) & 127), roll(value, 127))
            return (left + right) + (value + value)

        return line

    def sweep_planes(line, count, first_row, blocks, first, last, emit, unroll=2):
        starts = [first_row + 8 * b for b in range(blocks)]
        each = [(i, r) for i in range(count) for r in starts]
        before = [line(i, first - 1, r) for i, r in each]
        current = [line(i, first, r) for i, r in each]
        pair = [a + b for a, b in zip(before, current)]

        def body(index, carry):
            pair, current = carry
            for u in range(unroll):
                plane = first + unroll * index + u
                following = [line(i, plane + 1, r) for i, r in each]
                later = [a + b for a, b in zip(current, following)]
                sums = [a + b for a, b in zip(pair, later)]
                for b, r in enumerate(starts):
                    emit(u, index, plane, r, [sums[i * blocks + b] for i in range(count)])
                pair, current = later, following
            return tuple(pair), tuple(current)

        lax.fori_loop(0, (last - first) // unroll, body, (tuple(pair), tuple(current)))

    def slab_pass(edges, emit):
        for b in range(5):
            r = 4 + 8 * b
            sums = []
            for ref in edges:
                parts = [zsum(rows(ref, g, r)) for g in range(6)]
                up = [roll(p, 16) for p in parts]
                down = [roll(p, 112) for p in parts]
                sums.append([
                    (jnp.where(lane < 16, up[max(g - 1, 0)], up[g])
                     + jnp.where(lane >= 112, down[min(g + 1, 5)], down[g]))
                    + (parts[g] + parts[g])
                    for g in range(6)
                ])
            for g in range(6):
                emit(g, r, [s[g] for s in sums])

    def slab_ysum(ref, result):
        for g in range(6):
            for b in range(5):
                result[g, pl.ds(4 + 8 * b, 8), :] = ysum(ref, g, 4 + 8 * b)

    def first_emit(c, f, k, q, u, w, scale):
        def emit(_, __, plane, r, sums):
            at = (plane, pl.ds(r, 8), slice(None))
            centre = c[at]
            k[at] = 64.0 * centre + sums[0]
            factor = jnp.where(centre > 0.0, 1.0 / (48.0 * centre + sums[0]), 0.0)
            q[at] = factor
            if f is not None:
                value = (scale * factor) * f[at]
                u[at] = value
                w[at] = centre * value

        return emit

    def image_at(at, c, k, u, sums):
        return u[at] * k[at] - (c[at] * sums[0] + sums[1])

    def sweep_emit(c, f, k, q, u, tau, f_scale, u_out, w_out):
        def emit(_, __, plane, r, sums):
            at = (plane, pl.ds(r, 8), slice(None))
            rhs = f[at] if f_scale == 1.0 else f_scale * f[at]
            value = u[at] + (tau * q[at]) * (rhs - image_at(at, c, k, u, sums))
            u_out[at] = value
            if w_out is not None:
                w_out[at] = c[at] * value

        return emit

    def residual_emit(c, f, k, u, f_scale, low_row, result):
        held = {}

        def emit(step, index, plane, r, sums):
            at = (plane, pl.ds(r, 8), slice(None))
            rhs = f[at] if f_scale == 1.0 else f_scale * f[at]
            value = rhs - image_at(at, c, k, u, sums)
            if step == 0:
                held[r] = value
            else:
                result[index, pl.ds(r - low_row, 8), :] = halved(held[r] + value)

        return emit

    def slabbed(emit):
        return lambda g, r, sums: emit(0, 0, g, r, sums)

    arrive(msg_c, msg_f)

    def build_slab(ref, left, right, slab):
        def put(g, first, ks):
            for b in range(5):
                r = 4 + 8 * b
                middle = packed(ref, first, ks, r)
                slab[g, pl.ds(r, 8), :] = jnp.where(
                    group < 4, roll(rows(left, g, r), 120),
                    jnp.where(group < 12, middle, roll(rows(right, g, r), 8)),
                )

        put(0, -4, range(4, 8))

        @pl.loop(1, 5)
        def _(g):
            put(g, 8 * g - 4, range(8))

        put(5, 36, range(4))

    build_slab(c0, ocl, ocr, sc)
    build_slab(f0, ofl, ofr, sf)
    slab_ysum(sc, yc)
    slab_pass([yc], slabbed(first_emit(sc, sf, sk, sq, sua, swa, 8.0 * tau2[0])))
    slab_ysum(sua, yu)
    slab_ysum(swa, yw)
    sweep_planes(edged([c0], [yc]), 1, 4, 5, 1, 39, first_emit(c0, f0, k0, q0, ua, wa, 8.0 * tau2[0]))
    sweep_planes(edged([ua, wa], [yu, yw]), 2, 4, 5, 2, 38, sweep_emit(c0, f0, k0, q0, ua, tau2[1], 8.0, ub, wb))
    slab_pass([yu, yw], slabbed(sweep_emit(sc, sf, sk, sq, sua, tau2[1], 8.0, sub, swb)))
    slab_ysum(sub, yu)
    slab_ysum(swb, yw)
    sweep_planes(edged([ub, wb], [yu, yw]), 2, ROW, 4, 4, 36, residual_emit(c0, f0, k0, ub, 8.0, ROW, t0))

    @pl.loop(0, 16)
    def _(i):
        for b in range(2):
            total = t0[i, pl.ds(16 * b, 8, stride=2), :] + t0[i, pl.ds(16 * b + 1, 8, stride=2), :]
            f1[PX1 + i, pl.ds(ROW + 8 * b, 8), :] = jnp.where(own1, 0.5 * pick(total, down1), 0.0)

    pack_coarse(f1, of1, 16, LANE1)
    start(msg_f1)

    def merge(own, left, right, size, width, starts, low, put):
        lanes = size * 4
        at_left = jnp.logical_and(lane >= low - 8, lane < low)
        at_right = jnp.logical_and(lane >= low + lanes, lane < low + lanes + 8)

        def planes(g, ks):
            for k in ks:
                plane = 8 * g + k - 2
                for r in starts:
                    value = jnp.where(at_left, roll(rows(left, g, r), (low - 16 - 16 * k) % 128), rows(own, plane, r))
                    put(plane, r, jnp.where(at_right, roll(rows(right, g, r), (low + lanes - 16 * k) % 128), value))

        planes(0, range(8 - width, 8))
        for g in range(1, 1 + size // 8):
            planes(g, range(8))
        planes(1 + size // 8, range(width))

    def keep(result):
        def put(plane, r, value):
            result[plane, pl.ds(r, 8), :] = value

        return put

    def first_sweep(c, f, q, u, w, tau):
        def put(plane, r, value):
            at = (plane, pl.ds(r, 8), slice(None))
            f[at] = value
            value = (tau * q[at]) * value
            u[at] = value
            w[at] = c[at] * value

        return put

    arrive(msg_c1, msg_c2)
    merge(c1, ocl1, ocr1, 16, W_C1, range(0, 32, 8), LANE1, keep(cm1))
    merge(c2, ocl2, ocr2, 8, W_C2, range(2, 26, 8), LANE2, keep(cm2))
    sweep_planes(plain([cm1]), 1, 4, 3, 2, 26, first_emit(cm1, None, k1, q1, None, None, None))
    sweep_planes(plain([cm2]), 1, 3, 3, 1, 19, first_emit(cm2, None, k2, q2, None, None, None))

    arrive(msg_f1)
    merge(f1, ofl1, ofr1, 16, W_F1, range(4, 28, 8), LANE1, first_sweep(cm1, fm1, q1, ua1, wa1, tau2[0]))
    sweep_planes(plain([ua1, wa1]), 2, 4, 3, 3, 25, sweep_emit(cm1, fm1, k1, q1, ua1, tau2[1], 1.0, ub1, wb1))
    sweep_planes(plain([ub1, wb1]), 2, ROW, 2, 6, 22, residual_emit(cm1, fm1, k1, ub1, 1.0, ROW, t1))

    @pl.loop(0, 8)
    def _(i):
        total = t1[i, pl.ds(0, 8, stride=2), :] + t1[i, pl.ds(1, 8, stride=2), :]
        f2[PX1 + i, pl.ds(ROW, 8), :] = jnp.where(own2, 0.5 * pick(total, down2), 0.0)

    pack_coarse(f2, of2, 8, LANE2)
    start(msg_f2)

    arrive(msg_f2)
    merge(f2, ofl2, ofr2, 8, W_F2, range(3, 27, 8), LANE2, first_sweep(cm2, fm2, q2, ua2, wa2, tau4[0]))
    sweep_planes(plain([ua2, wa2]), 2, 4, 2, 2, 18, sweep_emit(cm2, fm2, k2, q2, ua2, tau4[1], 1.0, ub2, wb2))
    sweep_planes(plain([ub2, wb2]), 2, 4, 2, 3, 17, sweep_emit(cm2, fm2, k2, q2, ub2, tau4[2], 1.0, ua2, wa2))
    sweep_planes(plain([ua2, wa2]), 2, 4, 2, 4, 16, sweep_emit(cm2, fm2, k2, q2, ua2, tau4[3], 1.0, ub2, None))

    up = 32 + (lane >> 1)

    @pl.loop(0, 12)
    def _(i):
        for b in range(2):
            value = pick(rows(ub2, 4 + i, 6 + 8 * b), up)
            p1s[i, pl.ds(16 * b, 8, stride=2), :] = value
            p1s[i, pl.ds(16 * b + 1, 8, stride=2), :] = value

    @pl.loop(0, 12)
    def _(i):
        for dx in range(2):
            for b in range(3):
                at = (2 + 2 * i + dx, pl.ds(4 + 8 * b, 8), slice(None))
                value = ub1[at] + p1s[i, pl.ds(8 * b, 8), :]
                ua1[at] = value
                wa1[at] = cm1[at] * value

    sweep_planes(plain([ua1, wa1]), 2, 4, 3, 4, 24, sweep_emit(cm1, fm1, k1, q1, ua1, tau2[0], 1.0, ub1, wb1))
    sweep_planes(plain([ub1, wb1]), 2, 4, 3, 5, 23, sweep_emit(cm1, fm1, k1, q1, ub1, tau2[1], 1.0, ua1, None))

    side = 32 + ((group - 4 + jnp.where(group >= 8, 120, 0)) >> 1)

    @pl.loop(0, 18)
    def _(i):
        for b in range(3):
            value = pick(rows(ua1, 5 + i, 6 + 8 * b), up)
            p0s[i, pl.ds(16 * b, 8, stride=2), :] = value
            p0s[i, pl.ds(16 * b + 1, 8, stride=2), :] = value

    @pl.loop(0, 18)
    def _(i):
        for dx in range(2):
            for b in range(5):
                at = (2 + 2 * i + dx, pl.ds(4 + 8 * b, 8), slice(None))
                value = ub[at] + p0s[i, pl.ds(8 * b, 8), :]
                ua[at] = value
                wa[at] = c0[at] * value

    @pl.loop(0, 6)
    def _(g):
        for b in range(3):
            total = jnp.zeros((8, 128), F32)
            for m in range(4):
                total = jnp.where((lane >> 5) == m, pick(rows(ua1, 4 * g + 2 + m, 6 + 8 * b), side), total)
            sp[g, pl.ds(16 * b, 8, stride=2), :] = total
            sp[g, pl.ds(16 * b + 1, 8, stride=2), :] = total
        for b in range(5):
            at = (g, pl.ds(4 + 8 * b, 8), slice(None))
            value = sub[at] + sp[g, pl.ds(8 * b, 8), :]
            sua[at] = value
            swa[at] = sc[at] * value

    slab_ysum(sua, yu)
    slab_ysum(swa, yw)
    sweep_planes(edged([ua, wa], [yu, yw]), 2, 4, 5, 3, 37, sweep_emit(c0, f0, k0, q0, ua, tau2[0], 8.0, ub, wb))
    slab_pass([yu, yw], slabbed(sweep_emit(sc, sf, sk, sq, sua, tau2[0], 8.0, sub, swb)))
    slab_ysum(sub, yu)
    slab_ysum(swb, yw)

    def last_emit(_, __, plane, r, sums):
        at = (plane, pl.ds(r, 8), slice(None))
        value = ub[at] + (tau2[1] * q0[at]) * (8.0 * f0[at] - image_at(at, c0, k0, ub, sums))
        out_ref[plane - PX0, pl.ds(r - ROW, 8), :] = value

    sweep_planes(edged([ub, wb], [yu, yw]), 2, ROW, 4, 4, 36, last_emit)

    sent(msg_c, msg_f, msg_c1, msg_c2, msg_f1, msg_f2)


def solution(mesh):
    shape = tuple(mesh.shape[a] for a in ("gx", "gy", "gz"))
    count = 26 * 6
    big = [pltpu.VMEM((40, 48, 128), F32)] * 8
    slabs = [pltpu.VMEM((6, 48, 128), F32)] * 18
    level1 = [pltpu.VMEM((28, 32, 128), F32)] * 10 + [pltpu.VMEM((4, 32, 128), F32)] * 6
    level2 = [pltpu.VMEM((20, 32, 128), F32)] * 10 + [pltpu.VMEM((3, 32, 128), F32)] * 6
    between = [
        pltpu.VMEM((16, 32, 128), F32), pltpu.VMEM((18, 48, 128), F32),
        pltpu.VMEM((8, 16, 128), F32), pltpu.VMEM((12, 32, 128), F32),
    ]

    def per_device(right_side, coefficient):
        return pl.pallas_call(
            functools.partial(kernel, shape),
            out_shape=jax.ShapeDtypeStruct(right_side.shape, F32),
            in_specs=[pl.BlockSpec(memory_space=pl.ANY)] * 2,
            out_specs=pl.BlockSpec(memory_space=pltpu.VMEM),
            scratch_shapes=big + slabs + between + level1 + level2 + [
                pltpu.SemaphoreType.DMA((2,)),
                pltpu.SemaphoreType.DMA((count,)),
                pltpu.SemaphoreType.DMA((count,)),
            ],
            compiler_params=pltpu.CompilerParams(collective_id=0, has_side_effects=True),
        )(right_side, coefficient)

    placed = P("gx", "gy", "gz")
    return jax.shard_map(per_device, mesh=mesh, in_specs=(placed, placed), out_specs=placed, check_vma=False)
```

```python
import functools
import math

import jax
import jax.numpy as jnp
from jax import lax
from jax.experimental import pallas as pl
from jax.experimental.pallas import tpu as pltpu
from jax.sharding import PartitionSpec as P

MESH = pl.DeviceIdType.MESH
F32 = jnp.float32

PX0, ROW = 4, 8
PX1 = 6
U0, U1, U2 = 8, 8, 8
W_C0, W_F0, W_C1, W_C2, W_F1, W_F2 = 4, 3, 5, 6, 4, 5
LANE1, LANE2 = 32, 48

DIRS = [(a, b, c) for a in (-1, 0, 1) for b in (-1, 0, 1) for c in (-1, 0, 1) if (a, b, c) != (0, 0, 0)]
FLAT = [d for d in DIRS if d[2] == 0]
DEEP = [d for d in DIRS if d[2] != 0]


def step_sizes(sweeps):
    return [1.0 / (1.15 + 0.85 * math.cos(math.pi * (2 * j + 1) / (2 * sweeps))) for j in range(sweeps)]


def cut(step, low, size, width):
    if step == 0:
        return pl.ds(low, size), pl.ds(low, size)
    if step > 0:
        return pl.ds(low + size - width, width), pl.ds(low - width, width)
    return pl.ds(low, width), pl.ds(low + size, width)


def kernel(
    shape, right_hbm, coef_hbm, out_ref,
    c0, f0, k0, q0, ua, wa, ub, wb,
    oc, ocl, ocr, of, ofl, ofr,
    sc, sf, sk, sq, sua, swa, sub, swb, yc, yu, yw, ec, eu, ew, sp,
    t0, p0s, t1, p1s,
    c1, f1, cm1, fm1, k1, q1, ua1, wa1, ub1, wb1,
    oc1, ocl1, ocr1, of1, ofl1, ofr1,
    c2, f2, cm2, fm2, k2, q2, ua2, wa2, ub2, wb2,
    oc2, ocl2, ocr2, of2, ofl2, ofr2,
    in_sem, send_sem, recv_sem,
):
    spot = [lax.axis_index(a) for a in ("gx", "gy", "gz")]
    below = [s > 0 for s in spot]
    above = [s < n - 1 for s, n in zip(spot, shape)]

    def exists(d):
        found = None
        for axis, step in enumerate(d):
            if step != 0:
                one = above[axis] if step > 0 else below[axis]
                found = one if found is None else jnp.logical_and(found, one)
        return found

    def opposite(d):
        return tuple(-s for s in d)

    def device(d):
        return tuple(s + step for s, step in zip(spot, d))

    lane = lax.broadcasted_iota(jnp.int32, (8, 128), 1)
    group = lane & 15
    tau2 = step_sizes(2)
    tau4 = step_sizes(4)

    def roll(value, shift):
        return pltpu.roll(value, shift, axis=1)

    def pick(value, index):
        return jnp.take_along_axis(value, index, axis=1, mode="promise_in_bounds")

    def rows(ref, plane, start):
        return ref[plane, pl.ds(start, 8), :]

    in_c = pltpu.make_async_copy(coef_hbm, c0.at[pl.ds(PX0, 32), pl.ds(ROW, 32)], in_sem.at[0])
    in_f = pltpu.make_async_copy(right_hbm, f0.at[pl.ds(PX0, 32), pl.ds(ROW, 32)], in_sem.at[1])
    in_c.start()
    in_f.start()

    barrier = pltpu.get_barrier_semaphore()
    for d in DIRS:
        @pl.when(exists(d))
        def _():
            pl.semaphore_signal(barrier, inc=1, device_id=device(d), device_id_type=MESH)

    zero = jnp.zeros((8, 128), F32)
    flat = [(c0, PX0, 32, 32), (f0, PX0, 32, 32), (c1, PX1, 16, 16), (f1, PX1, 16, 16), (c2, PX1, 8, 8), (f2, PX1, 8, 8)]
    lefts = [(ocl, 1, 4, 32), (ofl, 1, 4, 32), (ocl1, 1, 2, 16), (ofl1, 1, 2, 16), (ocl2, 1, 1, 8), (ofl2, 1, 1, 8)]
    rights = [(ocr, 1, 4, 32), (ofr, 1, 4, 32), (ocr1, 1, 2, 16), (ofr1, 1, 2, 16), (ocr2, 1, 1, 8), (ofr2, 1, 1, 8)]

    def clear(ref, first, last, starts):
        @pl.loop(first, last)
        def _(i):
            for r in starts:
                ref[i, pl.ds(r, 8), :] = zero

    for axis in range(3):
        for side, present in ((0, below[axis]), (1, above[axis])):
            @pl.when(jnp.logical_not(present))
            def _():
                if axis == 2:
                    for ref, low, size_x, size_y in (lefts, rights)[side]:
                        clear(ref, 0, 2 * low + size_x, range(0, size_y + 16, 8))
                else:
                    for ref, low, size_x, size_y in flat + lefts + rights:
                        if axis == 0:
                            first = (0, low + size_x)[side]
                            clear(ref, first, first + low, range(0, size_y + 16, 8))
                        else:
                            clear(ref, 0, 2 * low + size_x, [(0, 8 + size_y)[side]])

    counter = [0]

    def message(d, src, dst):
        slot = counter[0]
        counter[0] += 1
        return pltpu.make_async_remote_copy(
            src_ref=src, dst_ref=dst, send_sem=send_sem.at[slot], recv_sem=recv_sem.at[slot],
            device_id=device(d), device_id_type=MESH,
        )

    def flat_messages(own, low, size, width):
        found = {}
        for d in FLAT:
            from_x, to_x = cut(d[0], low, size, width)
            from_y, to_y = cut(d[1], ROW, size, width)
            found[d] = [message(d, own.at[from_x, from_y], own.at[to_x, to_y])]
        return found

    def slab_messages(own, left, right, size, width):
        found = {}
        for d in DEEP:
            from_x, to_x = cut(d[0], 1, size // 8, 1)
            from_y, to_y = cut(d[1], ROW, size, width)
            target = left if d[2] > 0 else right
            found[d] = [message(d, own.at[from_x, from_y], target.at[to_x, to_y])]
        return found

    def messages(own, low, slab, left, right, size, width):
        return {**flat_messages(own, low, size, width), **slab_messages(slab, left, right, size, width)}

    msg_c = messages(c0, PX0, oc, ocl, ocr, 32, W_C0)
    msg_f = messages(f0, PX0, of, ofl, ofr, 32, W_F0)
    msg_c1 = messages(c1, PX1, oc1, ocl1, ocr1, 16, W_C1)
    msg_c2 = messages(c2, PX1, oc2, ocl2, ocr2, 8, W_C2)
    msg_f1 = messages(f1, PX1, of1, ofl1, ofr1, 16, W_F1)
    msg_f2 = messages(f2, PX1, of2, ofl2, ofr2, 8, W_F2)

    far_first = sorted(DIRS, key=lambda d: -sum(abs(s) for s in d))

    def start(*groups):
        for d in far_first:
            @pl.when(exists(d))
            def _():
                for found in groups:
                    for copy in found[d]:
                        copy.start()

    def arrive(*groups):
        for d in DIRS:
            @pl.when(exists(opposite(d)))
            def _():
                for found in groups:
                    for copy in found[d]:
                        copy.wait_recv()

    def sent(*groups):
        for d in DIRS:
            @pl.when(exists(d))
            def _():
                for found in groups:
                    for copy in found[d]:
                        copy.wait_send()

    def packed(ref, first, ks, start_row):
        total = jnp.zeros((8, 128), F32)
        for k in ks:
            value = rows(ref, first + k, start_row)
            low = roll(value, 16 * k + 4)
            high = roll(value, (16 * k + 12) % 128)
            total = jnp.where((lane >> 2) == 4 * k + 1, low, total)
            total = jnp.where((lane >> 2) == 4 * k + 2, high, total)
        return total

    def pack_own(ref, slab):
        @pl.loop(0, 4)
        def _(g):
            for b in range(4):
                slab[1 + g, pl.ds(ROW + 8 * b, 8), :] = packed(ref, PX0 + 8 * g, range(8), ROW + 8 * b)

    def pack_coarse(ref, slab, size, low):
        width = size * 4
        for g in range(size // 8):
            for b in range(size // 8):
                total = jnp.zeros((8, 128), F32)
                for k in range(8):
                    value = rows(ref, PX1 + 8 * g + k, ROW + 8 * b)
                    total = jnp.where((lane >> 3) == 2 * k, roll(value, (16 * k - low) % 128), total)
                    total = jnp.where((lane >> 3) == 2 * k + 1, roll(value, (16 * k + 16 - low - width) % 128), total)
                slab[1 + g, pl.ds(ROW + 8 * b, 8), :] = total

    in_c.wait()
    pack_own(c0, oc)
    in_f.wait()
    pack_own(f0, of)
    pl.semaphore_wait(
        barrier,
        math.prod(1 + b.astype(jnp.int32) + a.astype(jnp.int32) for b, a in zip(below, above)) - 1,
    )
    start(msg_c)
    start(msg_f)

    def halved(value):
        return value + roll(value, 127)

    down1 = jnp.clip(2 * (lane - LANE1), 0, 127)
    own1 = jnp.logical_and(lane >= LANE1, lane < LANE1 + 64)
    down2 = jnp.clip(LANE1 + 2 * (lane - LANE2), 0, 127)
    own2 = jnp.logical_and(lane >= LANE2, lane < LANE2 + 32)

    @pl.loop(0, 4)
    def _(turn):
        for step in range(4):
            i = 4 * turn + step
            for b in range(2):
                total = None
                for dx in range(2):
                    for dy in range(2):
                        part = c0[PX0 + 2 * i + dx, pl.ds(ROW + 16 * b + dy, 8, stride=2), :]
                        total = part if total is None else total + part
                c1[PX1 + i, pl.ds(ROW + 8 * b, 8), :] = jnp.where(own1, 0.125 * pick(halved(total), down1), 0.0)

    @pl.loop(0, 2)
    def _(turn):
        for step in range(4):
            i = 4 * turn + step
            total = None
            for dx in range(2):
                for dy in range(2):
                    part = c1[PX1 + 2 * i + dx, pl.ds(ROW + dy, 8, stride=2), :]
                    total = part if total is None else total + part
            c2[PX1 + i, pl.ds(ROW, 8), :] = jnp.where(own2, 0.125 * pick(halved(total), down2), 0.0)

    pack_coarse(c1, oc1, 16, LANE1)
    pack_coarse(c2, oc2, 8, LANE2)
    start(msg_c1, msg_c2)

    def ysum(ref, plane, start_row):
        above_, here, below_ = (rows(ref, plane, start_row + s) for s in (-1, 0, 1))
        return (above_ + below_) + (here + here)

    def zsum(value):
        return (roll(value, 1) + roll(value, 127)) + (value + value)

    def plain(refs):
        def line(i, base, step, start_row):
            return zsum(ysum(refs[i], base + step, start_row))

        return line

    first_lane, last_lane = lane == 0, lane == 127

    def edged(refs, edges):
        def line(i, base, step, start_row):
            value = ysum(refs[i], base + step, start_row)
            if isinstance(base, int):
                g, k = divmod(base + step + 4, 8)
            else:
                g, k = ((base + 4) >> 3) + step // 8, step % 8
            edge = roll(rows(edges[i], g, start_row), 127 - 16 * k)
            left = jnp.where(first_lane, edge, roll(value, 1))
            right = jnp.where(last_lane, edge, roll(value, 127))
            return (left + right) + (value + value)

        return line

    def sweep_planes(line, count, first_row, blocks, first, last, emit, unroll=8, align=0):
        starts = [first_row + 8 * b for b in range(blocks)]
        each = [(i, r) for i in range(count) for r in starts]
        before = [line(i, first - 1, 0, r) for i, r in each]
        current = [line(i, first, 0, r) for i, r in each]
        pair = [a + b for a, b in zip(before, current)]

        def some(base, steps, carry):
            pair, current = carry
            for u in range(steps):
                following = [line(i, base, u + 1, r) for i, r in each]
                later = [a + b for a, b in zip(current, following)]
                sums = [a + b for a, b in zip(pair, later)]
                for b, r in enumerate(starts):
                    emit(base + u, r, [sums[i * blocks + b] for i in range(count)])
                pair, current = later, following
            return tuple(pair), tuple(current)

        head = -(first + align) % unroll if align else 0
        carry = some(first, head, (tuple(pair), tuple(current)))
        start_plane = first + head
        turns = (last - start_plane) // unroll
        if turns > 1:
            carry = lax.fori_loop(0, turns, lambda t, carry: some(start_plane + unroll * t, unroll, carry), carry)
        elif turns == 1:
            carry = some(start_plane, unroll, carry)
        rest = start_plane + turns * unroll
        some(rest, last - rest, carry)

    def slab_pass(edges, emit):
        for b in range(5):
            r = 4 + 8 * b
            sums = []
            for ref in edges:
                parts = [zsum(rows(ref, g, r)) for g in range(6)]
                up = [roll(p, 16) for p in parts]
                down = [roll(p, 112) for p in parts]
                sums.append([
                    (jnp.where(lane < 16, up[max(g - 1, 0)], up[g])
                     + jnp.where(lane >= 112, down[min(g + 1, 5)], down[g]))
                    + (parts[g] + parts[g])
                    for g in range(6)
                ])
            for g in range(6):
                emit(g, r, [s[g] for s in sums])

    def slab_ysum(ref, result, edge):
        for g in range(6):
            for b in range(5):
                value = ysum(ref, g, 4 + 8 * b)
                result[g, pl.ds(4 + 8 * b, 8), :] = value
                edge[g, pl.ds(4 + 8 * b, 8), :] = jnp.where(group == 1, roll(value, 126), roll(value, 116))

    def first_emit(c, f, k, q, u, w, scale):
        def emit(plane, r, sums):
            at = (plane, pl.ds(r, 8), slice(None))
            centre = c[at]
            k[at] = 64.0 * centre + sums[0]
            factor = jnp.where(centre > 0.0, 1.0 / (48.0 * centre + sums[0]), 0.0)
            q[at] = factor
            if f is not None:
                value = (scale * factor) * f[at]
                u[at] = value
                w[at] = centre * value

        return emit

    def image_at(at, c, k, u, sums):
        return u[at] * k[at] - (c[at] * sums[0] + sums[1])

    def sweep_emit(c, f, k, q, u, tau, f_scale, u_out, w_out):
        def emit(plane, r, sums):
            at = (plane, pl.ds(r, 8), slice(None))
            rhs = f[at] if f_scale == 1.0 else f_scale * f[at]
            value = u[at] + (tau * q[at]) * (rhs - image_at(at, c, k, u, sums))
            u_out[at] = value
            if w_out is not None:
                w_out[at] = c[at] * value

        return emit

    def residual_emit(c, f, k, u, f_scale, low_plane, low_row, result):
        held = {}

        def emit(plane, r, sums):
            at = (plane, pl.ds(r, 8), slice(None))
            rhs = f[at] if f_scale == 1.0 else f_scale * f[at]
            value = rhs - image_at(at, c, k, u, sums)
            if r not in held:
                held[r] = value
            else:
                result[(plane - low_plane) >> 1, pl.ds(r - low_row, 8), :] = halved(held.pop(r) + value)

        return emit

    def slabbed(emit):
        return emit

    arrive(msg_c, msg_f)

    def build_slab(ref, left, right, slab):
        def put(g, first, ks):
            for b in range(5):
                r = 4 + 8 * b
                middle = packed(ref, first, ks, r)
                slab[g, pl.ds(r, 8), :] = jnp.where(
                    group < 4, roll(rows(left, g, r), 120),
                    jnp.where(group < 12, middle, roll(rows(right, g, r), 8)),
                )

        put(0, -4, range(4, 8))

        @pl.loop(1, 5)
        def _(g):
            put(g, 8 * g - 4, range(8))

        put(5, 36, range(4))

    build_slab(c0, ocl, ocr, sc)
    build_slab(f0, ofl, ofr, sf)
    slab_ysum(sc, yc, ec)
    slab_pass([yc], slabbed(first_emit(sc, sf, sk, sq, sua, swa, 8.0 * tau2[0])))
    slab_ysum(sua, yu, eu)
    slab_ysum(swa, yw, ew)
    sweep_planes(edged([c0], [ec]), 1, 4, 5, 1, 39, first_emit(c0, f0, k0, q0, ua, wa, 8.0 * tau2[0]), U0, 4)
    sweep_planes(edged([ua, wa], [eu, ew]), 2, 4, 5, 2, 38, sweep_emit(c0, f0, k0, q0, ua, tau2[1], 8.0, ub, wb), U0, 4)
    slab_pass([yu, yw], slabbed(sweep_emit(sc, sf, sk, sq, sua, tau2[1], 8.0, sub, swb)))
    slab_ysum(sub, yu, eu)
    slab_ysum(swb, yw, ew)
    sweep_planes(edged([ub, wb], [eu, ew]), 2, ROW, 4, 4, 36, residual_emit(c0, f0, k0, ub, 8.0, PX0, ROW, t0), U0, 4)

    @pl.loop(0, 2)
    def _(turn):
        for step in range(8):
            i = 8 * turn + step
            for b in range(2):
                total = t0[i, pl.ds(16 * b, 8, stride=2), :] + t0[i, pl.ds(16 * b + 1, 8, stride=2), :]
                f1[PX1 + i, pl.ds(ROW + 8 * b, 8), :] = jnp.where(own1, 0.5 * pick(total, down1), 0.0)

    pack_coarse(f1, of1, 16, LANE1)
    start(msg_f1)

    sent(msg_c, msg_f, msg_c1, msg_c2)
    def merge(own, left, right, size, width, starts, low, put):
        lanes = size * 4
        at_left = jnp.logical_and(lane >= low - 8, lane < low)
        at_right = jnp.logical_and(lane >= low + lanes, lane < low + lanes + 8)

        def planes(g, ks):
            for k in ks:
                plane = 8 * g + k - 2
                for r in starts:
                    value = jnp.where(at_left, roll(rows(left, g, r), (low - 16 - 16 * k) % 128), rows(own, plane, r))
                    put(plane, r, jnp.where(at_right, roll(rows(right, g, r), (low + lanes - 16 * k) % 128), value))

        planes(0, range(8 - width, 8))
        for g in range(1, 1 + size // 8):
            planes(g, range(8))
        planes(1 + size // 8, range(width))

    def keep(result):
        def put(plane, r, value):
            result[plane, pl.ds(r, 8), :] = value

        return put

    def first_sweep(c, f, q, u, w, tau):
        def put(plane, r, value):
            at = (plane, pl.ds(r, 8), slice(None))
            f[at] = value
            value = (tau * q[at]) * value
            u[at] = value
            w[at] = c[at] * value

        return put

    arrive(msg_c1, msg_c2)
    merge(c1, ocl1, ocr1, 16, W_C1, range(0, 32, 8), LANE1, keep(cm1))
    merge(c2, ocl2, ocr2, 8, W_C2, range(2, 26, 8), LANE2, keep(cm2))
    sweep_planes(plain([cm1]), 1, 4, 3, 2, 26, first_emit(cm1, None, k1, q1, None, None, None))
    sweep_planes(plain([cm2]), 1, 3, 3, 1, 19, first_emit(cm2, None, k2, q2, None, None, None))

    arrive(msg_f1)
    merge(f1, ofl1, ofr1, 16, W_F1, range(4, 28, 8), LANE1, first_sweep(cm1, fm1, q1, ua1, wa1, tau2[0]))
    sweep_planes(plain([ua1, wa1]), 2, 4, 3, 3, 25, sweep_emit(cm1, fm1, k1, q1, ua1, tau2[1], 1.0, ub1, wb1), U1)
    sweep_planes(plain([ub1, wb1]), 2, ROW, 2, 6, 22, residual_emit(cm1, fm1, k1, ub1, 1.0, PX1, ROW, t1), U1)

    @pl.loop(0, 1)
    def _(turn):
        for step in range(8):
            i = 8 * turn + step
            total = t1[i, pl.ds(0, 8, stride=2), :] + t1[i, pl.ds(1, 8, stride=2), :]
            f2[PX1 + i, pl.ds(ROW, 8), :] = jnp.where(own2, 0.5 * pick(total, down2), 0.0)

    pack_coarse(f2, of2, 8, LANE2)
    start(msg_f2)

    sent(msg_f1)
    arrive(msg_f2)
    merge(f2, ofl2, ofr2, 8, W_F2, range(3, 27, 8), LANE2, first_sweep(cm2, fm2, q2, ua2, wa2, tau4[0]))
    sweep_planes(plain([ua2, wa2]), 2, 4, 2, 2, 18, sweep_emit(cm2, fm2, k2, q2, ua2, tau4[1], 1.0, ub2, wb2), U2)
    sweep_planes(plain([ub2, wb2]), 2, 4, 2, 3, 17, sweep_emit(cm2, fm2, k2, q2, ub2, tau4[2], 1.0, ua2, wa2), U2)
    sweep_planes(plain([ua2, wa2]), 2, 4, 2, 4, 16, sweep_emit(cm2, fm2, k2, q2, ua2, tau4[3], 1.0, ub2, None), U2)

    sent(msg_f2)

    up = 32 + (lane >> 1)

    @pl.loop(0, 2)
    def _(turn):
        for step in range(6):
            i = 6 * turn + step
            for b in range(2):
                value = pick(rows(ub2, 4 + i, 6 + 8 * b), up)
                p1s[i, pl.ds(16 * b, 8, stride=2), :] = value
                p1s[i, pl.ds(16 * b + 1, 8, stride=2), :] = value

    @pl.loop(0, 4)
    def _(turn):
        for step in range(3):
            i = 3 * turn + step
            for dx in range(2):
                for b in range(3):
                    at = (2 + 2 * i + dx, pl.ds(4 + 8 * b, 8), slice(None))
                    value = ub1[at] + p1s[i, pl.ds(8 * b, 8), :]
                    ua1[at] = value
                    wa1[at] = cm1[at] * value

    sweep_planes(plain([ua1, wa1]), 2, 4, 3, 4, 24, sweep_emit(cm1, fm1, k1, q1, ua1, tau2[0], 1.0, ub1, wb1), U1)
    sweep_planes(plain([ub1, wb1]), 2, 4, 3, 5, 23, sweep_emit(cm1, fm1, k1, q1, ub1, tau2[1], 1.0, ua1, None), U1)

    side = 32 + ((group - 4 + jnp.where(group >= 8, 120, 0)) >> 1)

    @pl.loop(0, 3)
    def _(turn):
        for step in range(6):
            i = 6 * turn + step
            for b in range(3):
                value = pick(rows(ua1, 5 + i, 6 + 8 * b), up)
                p0s[i, pl.ds(16 * b, 8, stride=2), :] = value
                p0s[i, pl.ds(16 * b + 1, 8, stride=2), :] = value

    @pl.loop(0, 18)
    def _(i):
        for dx in range(2):
            for b in range(5):
                at = (2 + 2 * i + dx, pl.ds(4 + 8 * b, 8), slice(None))
                value = ub[at] + p0s[i, pl.ds(8 * b, 8), :]
                ua[at] = value
                wa[at] = c0[at] * value

    @pl.loop(0, 6)
    def _(g):
        for b in range(3):
            total = jnp.zeros((8, 128), F32)
            for m in range(4):
                total = jnp.where((lane >> 5) == m, pick(rows(ua1, 4 * g + 2 + m, 6 + 8 * b), side), total)
            sp[g, pl.ds(16 * b, 8, stride=2), :] = total
            sp[g, pl.ds(16 * b + 1, 8, stride=2), :] = total
        for b in range(5):
            at = (g, pl.ds(4 + 8 * b, 8), slice(None))
            value = sub[at] + sp[g, pl.ds(8 * b, 8), :]
            sua[at] = value
            swa[at] = sc[at] * value

    slab_ysum(sua, yu, eu)
    slab_ysum(swa, yw, ew)
    sweep_planes(edged([ua, wa], [eu, ew]), 2, 4, 5, 3, 37, sweep_emit(c0, f0, k0, q0, ua, tau2[0], 8.0, ub, wb), U0, 4)
    slab_pass([yu, yw], slabbed(sweep_emit(sc, sf, sk, sq, sua, tau2[0], 8.0, sub, swb)))
    slab_ysum(sub, yu, eu)
    slab_ysum(swb, yw, ew)

    def last_emit(plane, r, sums):
        at = (plane, pl.ds(r, 8), slice(None))
        value = ub[at] + (tau2[1] * q0[at]) * (8.0 * f0[at] - image_at(at, c0, k0, ub, sums))
        out_ref[plane - PX0, pl.ds(r - ROW, 8), :] = value

    sweep_planes(edged([ub, wb], [eu, ew]), 2, ROW, 4, 4, 36, last_emit, U0, 4)


def solution(mesh):
    shape = tuple(mesh.shape[a] for a in ("gx", "gy", "gz"))
    count = 26 * 6
    big = [pltpu.VMEM((40, 48, 128), F32)] * 8
    slabs = [pltpu.VMEM((6, 48, 128), F32)] * 21
    level1 = [pltpu.VMEM((28, 32, 128), F32)] * 10 + [pltpu.VMEM((4, 32, 128), F32)] * 6
    level2 = [pltpu.VMEM((20, 32, 128), F32)] * 10 + [pltpu.VMEM((3, 32, 128), F32)] * 6
    between = [
        pltpu.VMEM((16, 32, 128), F32), pltpu.VMEM((18, 48, 128), F32),
        pltpu.VMEM((8, 16, 128), F32), pltpu.VMEM((12, 32, 128), F32),
    ]

    def per_device(right_side, coefficient):
        return pl.pallas_call(
            functools.partial(kernel, shape),
            out_shape=jax.ShapeDtypeStruct(right_side.shape, F32),
            in_specs=[pl.BlockSpec(memory_space=pl.ANY)] * 2,
            out_specs=pl.BlockSpec(memory_space=pltpu.VMEM),
            scratch_shapes=big + slabs + between + level1 + level2 + [
                pltpu.SemaphoreType.DMA((2,)),
                pltpu.SemaphoreType.DMA((count,)),
                pltpu.SemaphoreType.DMA((count,)),
            ],
            compiler_params=pltpu.CompilerParams(collective_id=0, has_side_effects=True),
        )(right_side, coefficient)

    placed = P("gx", "gy", "gz")
    return jax.shard_map(per_device, mesh=mesh, in_specs=(placed, placed), out_specs=placed, check_vma=False)
```

```python
import functools
import math

import jax
import jax.numpy as jnp
from jax import lax
from jax.experimental import pallas as pl
from jax.experimental.pallas import tpu as pltpu
from jax.sharding import PartitionSpec as P

MESH = pl.DeviceIdType.MESH
F32 = jnp.float32

PX0, ROW = 4, 8
PX1 = 6
U0, U1, U2 = 8, 8, 8
W_C0, W_F0, W_C1, W_C2, W_F1, W_F2 = 4, 3, 5, 6, 4, 5
LANE1, LANE2 = 32, 48

DIRS = [(a, b, c) for a in (-1, 0, 1) for b in (-1, 0, 1) for c in (-1, 0, 1) if (a, b, c) != (0, 0, 0)]
FLAT = [d for d in DIRS if d[2] == 0]
DEEP = [d for d in DIRS if d[2] != 0]


def step_sizes(sweeps):
    return [1.0 / (1.15 + 0.85 * math.cos(math.pi * (2 * j + 1) / (2 * sweeps))) for j in range(sweeps)]


def cut(step, low, size, width):
    if step == 0:
        return pl.ds(low, size), pl.ds(low, size)
    if step > 0:
        return pl.ds(low + size - width, width), pl.ds(low - width, width)
    return pl.ds(low, width), pl.ds(low + size, width)


def kernel(
    shape, right_hbm, coef_hbm, out_ref,
    c0, f0, k0, q0, ua, wa, ub, wb,
    oc, ocl, ocr, of, ofl, ofr,
    sc, sf, sk, sq, sua, swa, sub, swb, yc, yu, yw, ec, eu, ew, sp,
    t0, p0s, t1, p1s,
    c1, f1, cm1, fm1, k1, q1, ua1, wa1, ub1, wb1,
    oc1, ocl1, ocr1, of1, ofl1, ofr1,
    c2, f2, cm2, fm2, k2, q2, ua2, wa2, ub2, wb2,
    oc2, ocl2, ocr2, of2, ofl2, ofr2,
    in_sem, send_sem, recv_sem,
):
    spot = [lax.axis_index(a) for a in ("gx", "gy", "gz")]
    below = [s > 0 for s in spot]
    above = [s < n - 1 for s, n in zip(spot, shape)]

    def exists(d):
        found = None
        for axis, step in enumerate(d):
            if step != 0:
                one = above[axis] if step > 0 else below[axis]
                found = one if found is None else jnp.logical_and(found, one)
        return found

    def opposite(d):
        return tuple(-s for s in d)

    def device(d):
        return tuple(s + step for s, step in zip(spot, d))

    lane = lax.broadcasted_iota(jnp.int32, (8, 128), 1)
    group = lane & 15
    tau2 = step_sizes(2)
    tau4 = step_sizes(4)

    def roll(value, shift):
        return pltpu.roll(value, shift, axis=1)

    def pick(value, index):
        return jnp.take_along_axis(value, index, axis=1, mode="promise_in_bounds")

    def rows(ref, plane, start):
        return ref[plane, pl.ds(start, 8), :]

    in_c = pltpu.make_async_copy(coef_hbm, c0.at[pl.ds(PX0, 32), pl.ds(ROW, 32)], in_sem.at[0])
    in_f = pltpu.make_async_copy(right_hbm, f0.at[pl.ds(PX0, 32), pl.ds(ROW, 32)], in_sem.at[1])
    in_c.start()
    in_f.start()

    far_first = sorted(DIRS, key=lambda d: -sum(abs(s) for s in d))

    barrier = pltpu.get_barrier_semaphore()
    for d in far_first:
        @pl.when(exists(d))
        def _():
            pl.semaphore_signal(barrier, inc=1, device_id=device(d), device_id_type=MESH)

    zero = jnp.zeros((8, 128), F32)
    flat = [(c0, PX0, 32, 32), (f0, PX0, 32, 32), (c1, PX1, 16, 16), (f1, PX1, 16, 16), (c2, PX1, 8, 8), (f2, PX1, 8, 8)]
    lefts = [(ocl, 1, 4, 32), (ofl, 1, 4, 32), (ocl1, 1, 2, 16), (ofl1, 1, 2, 16), (ocl2, 1, 1, 8), (ofl2, 1, 1, 8)]
    rights = [(ocr, 1, 4, 32), (ofr, 1, 4, 32), (ocr1, 1, 2, 16), (ofr1, 1, 2, 16), (ocr2, 1, 1, 8), (ofr2, 1, 1, 8)]

    def clear(ref, first, last, starts):
        @pl.loop(first, last)
        def _(i):
            for r in starts:
                ref[i, pl.ds(r, 8), :] = zero

    for axis in range(3):
        for side, present in ((0, below[axis]), (1, above[axis])):
            @pl.when(jnp.logical_not(present))
            def _():
                if axis == 2:
                    for ref, low, size_x, size_y in (lefts, rights)[side]:
                        clear(ref, 0, 2 * low + size_x, range(0, size_y + 16, 8))
                else:
                    for ref, low, size_x, size_y in flat + lefts + rights:
                        if axis == 0:
                            first = (0, low + size_x)[side]
                            clear(ref, first, first + low, range(0, size_y + 16, 8))
                        else:
                            clear(ref, 0, 2 * low + size_x, [(0, 8 + size_y)[side]])

    counter = [0]

    def message(d, src, dst):
        slot = counter[0]
        counter[0] += 1
        return pltpu.make_async_remote_copy(
            src_ref=src, dst_ref=dst, send_sem=send_sem.at[slot], recv_sem=recv_sem.at[slot],
            device_id=device(d), device_id_type=MESH,
        )

    def flat_messages(own, low, size, width):
        found = {}
        for d in FLAT:
            from_x, to_x = cut(d[0], low, size, width)
            from_y, to_y = cut(d[1], ROW, size, width)
            found[d] = [message(d, own.at[from_x, from_y], own.at[to_x, to_y])]
        return found

    def slab_messages(own, left, right, size, width):
        found = {}
        for d in DEEP:
            from_x, to_x = cut(d[0], 1, size // 8, 1)
            from_y, to_y = cut(d[1], ROW, size, width)
            target = left if d[2] > 0 else right
            found[d] = [message(d, own.at[from_x, from_y], target.at[to_x, to_y])]
        return found

    def messages(own, low, slab, left, right, size, width):
        return {**flat_messages(own, low, size, width), **slab_messages(slab, left, right, size, width)}

    msg_c = messages(c0, PX0, oc, ocl, ocr, 32, W_C0)
    msg_f = messages(f0, PX0, of, ofl, ofr, 32, W_F0)
    msg_c1 = messages(c1, PX1, oc1, ocl1, ocr1, 16, W_C1)
    msg_c2 = messages(c2, PX1, oc2, ocl2, ocr2, 8, W_C2)
    msg_f1 = messages(f1, PX1, of1, ofl1, ofr1, 16, W_F1)
    msg_f2 = messages(f2, PX1, of2, ofl2, ofr2, 8, W_F2)


    def start(*groups):
        for d in far_first:
            @pl.when(exists(d))
            def _():
                for found in groups:
                    for copy in found[d]:
                        copy.start()

    def arrive(*groups):
        for d in DIRS:
            @pl.when(exists(opposite(d)))
            def _():
                for found in groups:
                    for copy in found[d]:
                        copy.wait_recv()

    def sent(*groups):
        for d in DIRS:
            @pl.when(exists(d))
            def _():
                for found in groups:
                    for copy in found[d]:
                        copy.wait_send()

    def packed(ref, first, ks, start_row):
        total = jnp.zeros((8, 128), F32)
        for k in ks:
            value = rows(ref, first + k, start_row)
            low = roll(value, 16 * k + 4)
            high = roll(value, (16 * k + 12) % 128)
            total = jnp.where((lane >> 2) == 4 * k + 1, low, total)
            total = jnp.where((lane >> 2) == 4 * k + 2, high, total)
        return total

    def pack_own(ref, slab):
        for g in range(4):
            for b in range(4):
                slab[1 + g, pl.ds(ROW + 8 * b, 8), :] = packed(ref, PX0 + 8 * g, range(8), ROW + 8 * b)

    def pack_coarse(ref, slab, size, low):
        width = size * 4
        for g in range(size // 8):
            for b in range(size // 8):
                total = jnp.zeros((8, 128), F32)
                for k in range(8):
                    value = rows(ref, PX1 + 8 * g + k, ROW + 8 * b)
                    total = jnp.where((lane >> 3) == 2 * k, roll(value, (16 * k - low) % 128), total)
                    total = jnp.where((lane >> 3) == 2 * k + 1, roll(value, (16 * k + 16 - low - width) % 128), total)
                slab[1 + g, pl.ds(ROW + 8 * b, 8), :] = total

    in_c.wait()
    pack_own(c0, oc)
    in_f.wait()
    pack_own(f0, of)
    pl.semaphore_wait(
        barrier,
        math.prod(1 + b.astype(jnp.int32) + a.astype(jnp.int32) for b, a in zip(below, above)) - 1,
    )
    start(msg_c)
    start(msg_f)

    def halved(value):
        return value + roll(value, 127)

    down1 = jnp.clip(2 * (lane - LANE1), 0, 127)
    own1 = jnp.logical_and(lane >= LANE1, lane < LANE1 + 64)
    down2 = jnp.clip(LANE1 + 2 * (lane - LANE2), 0, 127)
    own2 = jnp.logical_and(lane >= LANE2, lane < LANE2 + 32)

    @pl.loop(0, 4)
    def _(turn):
        for step in range(4):
            i = 4 * turn + step
            for b in range(2):
                total = None
                for dx in range(2):
                    for dy in range(2):
                        part = c0[PX0 + 2 * i + dx, pl.ds(ROW + 16 * b + dy, 8, stride=2), :]
                        total = part if total is None else total + part
                c1[PX1 + i, pl.ds(ROW + 8 * b, 8), :] = jnp.where(own1, 0.125 * pick(halved(total), down1), 0.0)

    @pl.loop(0, 2)
    def _(turn):
        for step in range(4):
            i = 4 * turn + step
            total = None
            for dx in range(2):
                for dy in range(2):
                    part = c1[PX1 + 2 * i + dx, pl.ds(ROW + dy, 8, stride=2), :]
                    total = part if total is None else total + part
            c2[PX1 + i, pl.ds(ROW, 8), :] = jnp.where(own2, 0.125 * pick(halved(total), down2), 0.0)

    pack_coarse(c1, oc1, 16, LANE1)
    pack_coarse(c2, oc2, 8, LANE2)
    start(msg_c1, msg_c2)

    def ysum(ref, plane, start_row):
        above_, here, below_ = (rows(ref, plane, start_row + s) for s in (-1, 0, 1))
        return (above_ + below_) + (here + here)

    def zsum(value):
        return (roll(value, 1) + roll(value, 127)) + (value + value)

    def plain(refs):
        def line(i, base, step, start_row):
            return zsum(ysum(refs[i], base + step, start_row))

        return line

    first_lane, last_lane = lane == 0, lane == 127

    def edged(refs, edges):
        def line(i, base, step, start_row):
            value = ysum(refs[i], base + step, start_row)
            if isinstance(base, int):
                g, k = divmod(base + step + 4, 8)
            else:
                g, k = ((base + 4) >> 3) + step // 8, step % 8
            edge = roll(rows(edges[i], g, start_row), 127 - 16 * k)
            left = jnp.where(first_lane, edge, roll(value, 1))
            right = jnp.where(last_lane, edge, roll(value, 127))
            return (left + right) + (value + value)

        return line

    def sweep_planes(line, count, first_row, blocks, first, last, emit, unroll=8, align=0):
        starts = [first_row + 8 * b for b in range(blocks)]
        each = [(i, r) for i in range(count) for r in starts]
        before = [line(i, first - 1, 0, r) for i, r in each]
        current = [line(i, first, 0, r) for i, r in each]
        pair = [a + b for a, b in zip(before, current)]

        def some(base, steps, carry):
            pair, current = carry
            for u in range(steps):
                following = [line(i, base, u + 1, r) for i, r in each]
                later = [a + b for a, b in zip(current, following)]
                sums = [a + b for a, b in zip(pair, later)]
                for b, r in enumerate(starts):
                    emit(base + u, r, [sums[i * blocks + b] for i in range(count)])
                pair, current = later, following
            return tuple(pair), tuple(current)

        head = -(first + align) % unroll if align else 0
        carry = some(first, head, (tuple(pair), tuple(current)))
        start_plane = first + head
        turns = (last - start_plane) // unroll
        if turns > 1:
            carry = lax.fori_loop(0, turns, lambda t, carry: some(start_plane + unroll * t, unroll, carry), carry)
        elif turns == 1:
            carry = some(start_plane, unroll, carry)
        rest = start_plane + turns * unroll
        some(rest, last - rest, carry)

    def slab_pass(edges, emit):
        for b in range(5):
            r = 4 + 8 * b
            sums = []
            for ref in edges:
                parts = [zsum(rows(ref, g, r)) for g in range(6)]
                up = [roll(p, 16) for p in parts]
                down = [roll(p, 112) for p in parts]
                sums.append([
                    (jnp.where(lane < 16, up[max(g - 1, 0)], up[g])
                     + jnp.where(lane >= 112, down[min(g + 1, 5)], down[g]))
                    + (parts[g] + parts[g])
                    for g in range(6)
                ])
            for g in range(6):
                emit(g, r, [s[g] for s in sums])

    def slab_ysum(ref, result, edge):
        for g in range(6):
            for b in range(5):
                value = ysum(ref, g, 4 + 8 * b)
                result[g, pl.ds(4 + 8 * b, 8), :] = value
                edge[g, pl.ds(4 + 8 * b, 8), :] = jnp.where(group == 1, roll(value, 126), roll(value, 116))

    def factors_emit(c, k, q):
        def emit(plane, r, sums):
            at = (plane, pl.ds(r, 8), slice(None))
            centre = c[at]
            k[at] = 64.0 * centre + sums[0]
            q[at] = jnp.where(centre > 0.0, 1.0 / (48.0 * centre + sums[0]), 0.0)

        return emit

    def image_at(at, c, k, u, sums):
        return u[at] * k[at] - (c[at] * sums[0] + sums[1])

    def sweep_emit(c, f, k, q, u, tau, f_scale, u_out, w_out):
        def emit(plane, r, sums):
            at = (plane, pl.ds(r, 8), slice(None))
            rhs = f[at] if f_scale == 1.0 else f_scale * f[at]
            value = u[at] + (tau * q[at]) * (rhs - image_at(at, c, k, u, sums))
            u_out[at] = value
            if w_out is not None:
                w_out[at] = c[at] * value

        return emit

    def residual_emit(c, f, k, u, f_scale, low_plane, low_row, result):
        held = {}

        def emit(plane, r, sums):
            at = (plane, pl.ds(r, 8), slice(None))
            rhs = f[at] if f_scale == 1.0 else f_scale * f[at]
            value = rhs - image_at(at, c, k, u, sums)
            if r not in held:
                held[r] = value
            else:
                result[(plane - low_plane) >> 1, pl.ds(r - low_row, 8), :] = halved(held.pop(r) + value)

        return emit

    row = lax.broadcasted_iota(jnp.int32, (8, 128), 0)

    def build_slab(ref, own, left, right, slab):
        def join(low, middle, high):
            return jnp.where(group < 4, roll(low, 120), jnp.where(group < 12, middle, roll(high, 8)))

        def ends(ref, plane):
            return jnp.where(row < 4, rows(ref, plane, 4), rows(ref, plane, 36))

        def pack(load, first, ks):
            total = jnp.zeros((8, 128), F32)
            for k in ks:
                value = load(first + k)
                total = jnp.where((lane >> 2) == 4 * k + 1, roll(value, 16 * k + 4), total)
                total = jnp.where((lane >> 2) == 4 * k + 2, roll(value, (16 * k + 12) % 128), total)
            return total

        def put(g, first, ks, inner):
            for r in range(8, 40, 8):
                middle = rows(own, g, r) if inner else pack(lambda plane: rows(ref, plane, r), first, ks)
                slab[g, pl.ds(r, 8), :] = join(rows(left, g, r), middle, rows(right, g, r))
            outer = join(ends(left, g), pack(lambda plane: ends(ref, plane), first, ks), ends(right, g))
            slab[g, pl.ds(4, 4), :] = outer[0:4]
            slab[g, pl.ds(40, 4), :] = outer[4:8]

        put(0, -4, range(4, 8), False)
        for g in range(1, 5):
            put(g, 8 * g - 4, range(8), True)
        put(5, 36, range(4), False)

    arrive(msg_c)
    build_slab(c0, oc, ocl, ocr, sc)
    slab_ysum(sc, yc, ec)
    slab_pass([yc], factors_emit(sc, sk, sq))
    sweep_planes(edged([c0], [ec]), 1, 4, 5, 1, 39, factors_emit(c0, k0, q0), U0, 4)

    arrive(msg_f)
    build_slab(f0, of, ofl, ofr, sf)
    scale = 8.0 * tau2[0]
    for g in range(6):
        for b in range(5):
            at = (g, pl.ds(4 + 8 * b, 8), slice(None))
            value = (scale * sq[at]) * sf[at]
            sua[at] = value
            swa[at] = sc[at] * value
    slab_ysum(sua, yu, eu)
    slab_ysum(swa, yw, ew)

    @pl.loop(0, 19)
    def _(i):
        for dx in range(2):
            for b in range(5):
                at = (1 + 2 * i + dx, pl.ds(4 + 8 * b, 8), slice(None))
                value = (scale * q0[at]) * f0[at]
                ua[at] = value
                wa[at] = c0[at] * value

    sweep_planes(edged([ua, wa], [eu, ew]), 2, 4, 5, 2, 38, sweep_emit(c0, f0, k0, q0, ua, tau2[1], 8.0, ub, wb), U0, 4)
    slab_pass([yu, yw], (sweep_emit(sc, sf, sk, sq, sua, tau2[1], 8.0, sub, swb)))
    slab_ysum(sub, yu, eu)
    slab_ysum(swb, yw, ew)
    sweep_planes(edged([ub, wb], [eu, ew]), 2, ROW, 4, 4, 36, residual_emit(c0, f0, k0, ub, 8.0, PX0, ROW, t0), U0, 4)

    @pl.loop(0, 2)
    def _(turn):
        for step in range(8):
            i = 8 * turn + step
            for b in range(2):
                total = t0[i, pl.ds(16 * b, 8, stride=2), :] + t0[i, pl.ds(16 * b + 1, 8, stride=2), :]
                f1[PX1 + i, pl.ds(ROW + 8 * b, 8), :] = jnp.where(own1, 0.5 * pick(total, down1), 0.0)

    pack_coarse(f1, of1, 16, LANE1)
    start(msg_f1)

    sent(msg_c, msg_f, msg_c1, msg_c2)
    def merge(own, left, right, size, width, starts, low, put):
        lanes = size * 4
        at_left = jnp.logical_and(lane >= low - 8, lane < low)
        at_right = jnp.logical_and(lane >= low + lanes, lane < low + lanes + 8)

        def planes(g, ks):
            for k in ks:
                plane = 8 * g + k - 2
                for r in starts:
                    value = jnp.where(at_left, roll(rows(left, g, r), (low - 16 - 16 * k) % 128), rows(own, plane, r))
                    put(plane, r, jnp.where(at_right, roll(rows(right, g, r), (low + lanes - 16 * k) % 128), value))

        planes(0, range(8 - width, 8))
        for g in range(1, 1 + size // 8):
            planes(g, range(8))
        planes(1 + size // 8, range(width))

    def keep(result):
        def put(plane, r, value):
            result[plane, pl.ds(r, 8), :] = value

        return put

    def first_sweep(c, f, q, u, w, tau):
        def put(plane, r, value):
            at = (plane, pl.ds(r, 8), slice(None))
            f[at] = value
            value = (tau * q[at]) * value
            u[at] = value
            w[at] = c[at] * value

        return put

    arrive(msg_c1, msg_c2)
    merge(c1, ocl1, ocr1, 16, W_C1, range(0, 32, 8), LANE1, keep(cm1))
    merge(c2, ocl2, ocr2, 8, W_C2, range(2, 26, 8), LANE2, keep(cm2))
    sweep_planes(plain([cm1]), 1, 4, 3, 2, 26, factors_emit(cm1, k1, q1))
    sweep_planes(plain([cm2]), 1, 3, 3, 1, 19, factors_emit(cm2, k2, q2))

    arrive(msg_f1)
    merge(f1, ofl1, ofr1, 16, W_F1, range(4, 28, 8), LANE1, first_sweep(cm1, fm1, q1, ua1, wa1, tau2[0]))
    sweep_planes(plain([ua1, wa1]), 2, 4, 3, 3, 25, sweep_emit(cm1, fm1, k1, q1, ua1, tau2[1], 1.0, ub1, wb1), U1)
    sweep_planes(plain([ub1, wb1]), 2, ROW, 2, 6, 22, residual_emit(cm1, fm1, k1, ub1, 1.0, PX1, ROW, t1), U1)

    @pl.loop(0, 1)
    def _(turn):
        for step in range(8):
            i = 8 * turn + step
            total = t1[i, pl.ds(0, 8, stride=2), :] + t1[i, pl.ds(1, 8, stride=2), :]
            f2[PX1 + i, pl.ds(ROW, 8), :] = jnp.where(own2, 0.5 * pick(total, down2), 0.0)

    pack_coarse(f2, of2, 8, LANE2)
    start(msg_f2)

    sent(msg_f1)
    arrive(msg_f2)
    merge(f2, ofl2, ofr2, 8, W_F2, range(3, 27, 8), LANE2, first_sweep(cm2, fm2, q2, ua2, wa2, tau4[0]))
    sweep_planes(plain([ua2, wa2]), 2, 4, 2, 2, 18, sweep_emit(cm2, fm2, k2, q2, ua2, tau4[1], 1.0, ub2, wb2), U2)
    sweep_planes(plain([ub2, wb2]), 2, 4, 2, 3, 17, sweep_emit(cm2, fm2, k2, q2, ub2, tau4[2], 1.0, ua2, wa2), U2)
    sweep_planes(plain([ua2, wa2]), 2, 4, 2, 4, 16, sweep_emit(cm2, fm2, k2, q2, ua2, tau4[3], 1.0, ub2, None), U2)

    sent(msg_f2)

    up = 32 + (lane >> 1)

    @pl.loop(0, 2)
    def _(turn):
        for step in range(6):
            i = 6 * turn + step
            for b in range(2):
                value = pick(rows(ub2, 4 + i, 6 + 8 * b), up)
                p1s[i, pl.ds(16 * b, 8, stride=2), :] = value
                p1s[i, pl.ds(16 * b + 1, 8, stride=2), :] = value

    @pl.loop(0, 4)
    def _(turn):
        for step in range(3):
            i = 3 * turn + step
            for dx in range(2):
                for b in range(3):
                    at = (2 + 2 * i + dx, pl.ds(4 + 8 * b, 8), slice(None))
                    value = ub1[at] + p1s[i, pl.ds(8 * b, 8), :]
                    ua1[at] = value
                    wa1[at] = cm1[at] * value

    sweep_planes(plain([ua1, wa1]), 2, 4, 3, 4, 24, sweep_emit(cm1, fm1, k1, q1, ua1, tau2[0], 1.0, ub1, wb1), U1)
    sweep_planes(plain([ub1, wb1]), 2, 4, 3, 5, 23, sweep_emit(cm1, fm1, k1, q1, ub1, tau2[1], 1.0, ua1, None), U1)

    side = 32 + ((group - 4 + jnp.where(group >= 8, 120, 0)) >> 1)

    @pl.loop(0, 3)
    def _(turn):
        for step in range(6):
            i = 6 * turn + step
            for b in range(3):
                value = pick(rows(ua1, 5 + i, 6 + 8 * b), up)
                p0s[i, pl.ds(16 * b, 8, stride=2), :] = value
                p0s[i, pl.ds(16 * b + 1, 8, stride=2), :] = value

    @pl.loop(0, 18)
    def _(i):
        for dx in range(2):
            for b in range(5):
                at = (2 + 2 * i + dx, pl.ds(4 + 8 * b, 8), slice(None))
                value = ub[at] + p0s[i, pl.ds(8 * b, 8), :]
                ua[at] = value
                wa[at] = c0[at] * value

    @pl.loop(0, 6)
    def _(g):
        for b in range(3):
            total = jnp.zeros((8, 128), F32)
            for m in range(4):
                total = jnp.where((lane >> 5) == m, pick(rows(ua1, 4 * g + 2 + m, 6 + 8 * b), side), total)
            sp[g, pl.ds(16 * b, 8, stride=2), :] = total
            sp[g, pl.ds(16 * b + 1, 8, stride=2), :] = total
        for b in range(5):
            at = (g, pl.ds(4 + 8 * b, 8), slice(None))
            value = sub[at] + sp[g, pl.ds(8 * b, 8), :]
            sua[at] = value
            swa[at] = sc[at] * value

    slab_ysum(sua, yu, eu)
    slab_ysum(swa, yw, ew)
    sweep_planes(edged([ua, wa], [eu, ew]), 2, 4, 5, 3, 37, sweep_emit(c0, f0, k0, q0, ua, tau2[0], 8.0, ub, wb), U0, 4)
    slab_pass([yu, yw], (sweep_emit(sc, sf, sk, sq, sua, tau2[0], 8.0, sub, swb)))
    slab_ysum(sub, yu, eu)
    slab_ysum(swb, yw, ew)

    def last_emit(plane, r, sums):
        at = (plane, pl.ds(r, 8), slice(None))
        value = ub[at] + (tau2[1] * q0[at]) * (8.0 * f0[at] - image_at(at, c0, k0, ub, sums))
        out_ref[plane - PX0, pl.ds(r - ROW, 8), :] = value

    sweep_planes(edged([ub, wb], [eu, ew]), 2, ROW, 4, 4, 36, last_emit, U0, 4)


def solution(mesh):
    shape = tuple(mesh.shape[a] for a in ("gx", "gy", "gz"))
    count = 26 * 6
    big = [pltpu.VMEM((40, 48, 128), F32)] * 8
    slabs = [pltpu.VMEM((6, 48, 128), F32)] * 21
    level1 = [pltpu.VMEM((28, 32, 128), F32)] * 10 + [pltpu.VMEM((4, 32, 128), F32)] * 6
    level2 = [pltpu.VMEM((20, 32, 128), F32)] * 10 + [pltpu.VMEM((3, 32, 128), F32)] * 6
    between = [
        pltpu.VMEM((16, 32, 128), F32), pltpu.VMEM((18, 48, 128), F32),
        pltpu.VMEM((8, 16, 128), F32), pltpu.VMEM((12, 32, 128), F32),
    ]

    def per_device(right_side, coefficient):
        return pl.pallas_call(
            functools.partial(kernel, shape),
            out_shape=jax.ShapeDtypeStruct(right_side.shape, F32),
            in_specs=[pl.BlockSpec(memory_space=pl.ANY)] * 2,
            out_specs=pl.BlockSpec(memory_space=pltpu.VMEM),
            scratch_shapes=big + slabs + between + level1 + level2 + [
                pltpu.SemaphoreType.DMA((2,)),
                pltpu.SemaphoreType.DMA((count,)),
                pltpu.SemaphoreType.DMA((count,)),
            ],
            compiler_params=pltpu.CompilerParams(
                collective_id=0, has_side_effects=True, vmem_limit_bytes=24 * 1024 * 1024
            ),
        )(*(pltpu.with_memory_space_constraint(x, pltpu.HBM) for x in (right_side, coefficient)))

    placed = P("gx", "gy", "gz")
    return jax.shard_map(per_device, mesh=mesh, in_specs=(placed, placed), out_specs=placed, check_vma=False)
```

```python
import functools
import math

import jax
import jax.numpy as jnp
from jax import lax
from jax.experimental import pallas as pl
from jax.experimental.pallas import tpu as pltpu
from jax.sharding import PartitionSpec as P

MESH = pl.DeviceIdType.MESH
F32 = jnp.float32

PX0, ROW = 4, 8
PX1 = 6
U0, U1, U2 = 16, 12, 16
W_C0, W_F0, W_C1, W_C2, W_F1, W_F2 = 4, 3, 5, 6, 4, 5
LANE1, LANE2 = 32, 48

DIRS = [(a, b, c) for a in (-1, 0, 1) for b in (-1, 0, 1) for c in (-1, 0, 1) if (a, b, c) != (0, 0, 0)]
FLAT = [d for d in DIRS if d[2] == 0]
DEEP = [d for d in DIRS if d[2] != 0]


def step_sizes(sweeps):
    return [1.0 / (1.15 + 0.85 * math.cos(math.pi * (2 * j + 1) / (2 * sweeps))) for j in range(sweeps)]


def cut(step, low, size, width):
    if step == 0:
        return pl.ds(low, size), pl.ds(low, size)
    if step > 0:
        return pl.ds(low + size - width, width), pl.ds(low - width, width)
    return pl.ds(low, width), pl.ds(low + size, width)


def kernel(
    shape, right_hbm, coef_hbm, out_ref,
    c0, f0, k0, q0, ua, wa, ub, wb,
    oc, ocl, ocr, of, ofl, ofr,
    sc, sf, sk, sq, sua, swa, sub, swb, yc, yu, yw, ec, eu, ew, sp,
    t0, p0s, t1, p1s,
    c1, f1, cm1, fm1, k1, q1, ua1, wa1, ub1, wb1,
    oc1, ocl1, ocr1, of1, ofl1, ofr1,
    c2, f2, cm2, fm2, k2, q2, ua2, wa2, ub2, wb2,
    oc2, ocl2, ocr2, of2, ofl2, ofr2,
    in_sem, send_sem, recv_sem,
):
    spot = [lax.axis_index(a) for a in ("gx", "gy", "gz")]
    below = [s > 0 for s in spot]
    above = [s < n - 1 for s, n in zip(spot, shape)]

    def exists(d):
        found = None
        for axis, step in enumerate(d):
            if step != 0:
                one = above[axis] if step > 0 else below[axis]
                found = one if found is None else jnp.logical_and(found, one)
        return found

    def opposite(d):
        return tuple(-s for s in d)

    def device(d):
        return tuple(s + step for s, step in zip(spot, d))

    lane = lax.broadcasted_iota(jnp.int32, (8, 128), 1)
    group = lane & 15
    tau2 = step_sizes(2)
    tau4 = step_sizes(4)

    def roll(value, shift):
        return pltpu.roll(value, shift, axis=1)

    def pick(value, index):
        return jnp.take_along_axis(value, index, axis=1, mode="promise_in_bounds")

    def rows(ref, plane, start):
        return ref[plane, pl.ds(start, 8), :]

    in_c = pltpu.make_async_copy(coef_hbm, c0.at[pl.ds(PX0, 32), pl.ds(ROW, 32)], in_sem.at[0])
    in_f = pltpu.make_async_copy(right_hbm, f0.at[pl.ds(PX0, 32), pl.ds(ROW, 32)], in_sem.at[1])
    in_c.start()
    in_f.start()

    far_first = sorted(DIRS, key=lambda d: -sum(abs(s) for s in d))

    barrier = pltpu.get_barrier_semaphore()
    for d in far_first:
        @pl.when(exists(d))
        def _():
            pl.semaphore_signal(barrier, inc=1, device_id=device(d), device_id_type=MESH)

    zero = jnp.zeros((8, 128), F32)
    flat = [(c0, PX0, 32, 32), (f0, PX0, 32, 32), (c1, PX1, 16, 16), (f1, PX1, 16, 16), (c2, PX1, 8, 8), (f2, PX1, 8, 8)]
    lefts = [(ocl, 1, 4, 32), (ofl, 1, 4, 32), (ocl1, 1, 2, 16), (ofl1, 1, 2, 16), (ocl2, 1, 1, 8), (ofl2, 1, 1, 8)]
    rights = [(ocr, 1, 4, 32), (ofr, 1, 4, 32), (ocr1, 1, 2, 16), (ofr1, 1, 2, 16), (ocr2, 1, 1, 8), (ofr2, 1, 1, 8)]

    def clear(ref, first, last, starts):
        @pl.loop(first, last)
        def _(i):
            for r in starts:
                ref[i, pl.ds(r, 8), :] = zero

    for axis in range(3):
        for side, present in ((0, below[axis]), (1, above[axis])):
            @pl.when(jnp.logical_not(present))
            def _():
                if axis == 2:
                    for ref, low, size_x, size_y in (lefts, rights)[side]:
                        clear(ref, 0, 2 * low + size_x, range(0, size_y + 16, 8))
                else:
                    for ref, low, size_x, size_y in flat + lefts + rights:
                        if axis == 0:
                            first = (0, low + size_x)[side]
                            clear(ref, first, first + low, range(0, size_y + 16, 8))
                        else:
                            clear(ref, 0, 2 * low + size_x, [(0, 8 + size_y)[side]])

    counter = [0]

    def message(d, src, dst):
        slot = counter[0]
        counter[0] += 1
        return pltpu.make_async_remote_copy(
            src_ref=src, dst_ref=dst, send_sem=send_sem.at[slot], recv_sem=recv_sem.at[slot],
            device_id=device(d), device_id_type=MESH,
        )

    def flat_messages(own, low, size, width):
        found = {}
        for d in FLAT:
            from_x, to_x = cut(d[0], low, size, width)
            from_y, to_y = cut(d[1], ROW, size, width)
            found[d] = [message(d, own.at[from_x, from_y], own.at[to_x, to_y])]
        return found

    def slab_messages(own, left, right, size, width):
        found = {}
        for d in DEEP:
            from_x, to_x = cut(d[0], 1, size // 8, 1)
            from_y, to_y = cut(d[1], ROW, size, width)
            target = left if d[2] > 0 else right
            found[d] = [message(d, own.at[from_x, from_y], target.at[to_x, to_y])]
        return found

    def messages(own, low, slab, left, right, size, width):
        return {**flat_messages(own, low, size, width), **slab_messages(slab, left, right, size, width)}

    msg_c = messages(c0, PX0, oc, ocl, ocr, 32, W_C0)
    msg_f = messages(f0, PX0, of, ofl, ofr, 32, W_F0)
    msg_c1 = messages(c1, PX1, oc1, ocl1, ocr1, 16, W_C1)
    msg_c2 = messages(c2, PX1, oc2, ocl2, ocr2, 8, W_C2)
    msg_f1 = messages(f1, PX1, of1, ofl1, ofr1, 16, W_F1)
    msg_f2 = messages(f2, PX1, of2, ofl2, ofr2, 8, W_F2)


    def start(*groups):
        for d in far_first:
            @pl.when(exists(d))
            def _():
                for found in groups:
                    for copy in found[d]:
                        copy.start()

    def arrive(*groups):
        for d in DIRS:
            @pl.when(exists(opposite(d)))
            def _():
                for found in groups:
                    for copy in found[d]:
                        copy.wait_recv()

    def sent(*groups):
        for d in DIRS:
            @pl.when(exists(d))
            def _():
                for found in groups:
                    for copy in found[d]:
                        copy.wait_send()

    def packed(ref, first, ks, start_row):
        total = jnp.zeros((8, 128), F32)
        for k in ks:
            value = rows(ref, first + k, start_row)
            low = roll(value, 16 * k + 4)
            high = roll(value, (16 * k + 12) % 128)
            total = jnp.where((lane >> 2) == 4 * k + 1, low, total)
            total = jnp.where((lane >> 2) == 4 * k + 2, high, total)
        return total

    def pack_own(ref, slab):
        for g in range(4):
            for b in range(4):
                slab[1 + g, pl.ds(ROW + 8 * b, 8), :] = packed(ref, PX0 + 8 * g, range(8), ROW + 8 * b)

    def pack_coarse(ref, slab, size, low):
        width = size * 4
        for g in range(size // 8):
            for b in range(size // 8):
                total = jnp.zeros((8, 128), F32)
                for k in range(8):
                    value = rows(ref, PX1 + 8 * g + k, ROW + 8 * b)
                    total = jnp.where((lane >> 3) == 2 * k, roll(value, (16 * k - low) % 128), total)
                    total = jnp.where((lane >> 3) == 2 * k + 1, roll(value, (16 * k + 16 - low - width) % 128), total)
                slab[1 + g, pl.ds(ROW + 8 * b, 8), :] = total

    in_c.wait()
    pack_own(c0, oc)
    in_f.wait()
    pack_own(f0, of)
    pl.semaphore_wait(
        barrier,
        math.prod(1 + b.astype(jnp.int32) + a.astype(jnp.int32) for b, a in zip(below, above)) - 1,
    )
    start(msg_c)
    start(msg_f)

    def halved(value):
        return value + roll(value, 127)

    down1 = jnp.clip(2 * (lane - LANE1), 0, 127)
    own1 = jnp.logical_and(lane >= LANE1, lane < LANE1 + 64)
    down2 = jnp.clip(LANE1 + 2 * (lane - LANE2), 0, 127)
    own2 = jnp.logical_and(lane >= LANE2, lane < LANE2 + 32)

    @pl.loop(0, 4)
    def _(turn):
        for step in range(4):
            i = 4 * turn + step
            for b in range(2):
                total = None
                for dx in range(2):
                    for dy in range(2):
                        part = c0[PX0 + 2 * i + dx, pl.ds(ROW + 16 * b + dy, 8, stride=2), :]
                        total = part if total is None else total + part
                c1[PX1 + i, pl.ds(ROW + 8 * b, 8), :] = jnp.where(own1, 0.125 * pick(halved(total), down1), 0.0)

    @pl.loop(0, 2)
    def _(turn):
        for step in range(4):
            i = 4 * turn + step
            total = None
            for dx in range(2):
                for dy in range(2):
                    part = c1[PX1 + 2 * i + dx, pl.ds(ROW + dy, 8, stride=2), :]
                    total = part if total is None else total + part
            c2[PX1 + i, pl.ds(ROW, 8), :] = jnp.where(own2, 0.125 * pick(halved(total), down2), 0.0)

    pack_coarse(c1, oc1, 16, LANE1)
    pack_coarse(c2, oc2, 8, LANE2)
    start(msg_c1, msg_c2)

    def ysum(ref, plane, start_row):
        above_, here, below_ = (rows(ref, plane, start_row + s) for s in (-1, 0, 1))
        return (above_ + below_) + (here + here)

    def zsum(value):
        return (roll(value, 1) + roll(value, 127)) + (value + value)

    def plain(refs):
        def line(i, base, step, start_row):
            return zsum(ysum(refs[i], base + step, start_row))

        return line

    first_lane, last_lane = lane == 0, lane == 127

    def edged(refs, edges):
        def line(i, base, step, start_row):
            value = ysum(refs[i], base + step, start_row)
            if isinstance(base, int):
                g, k = divmod(base + step + 4, 8)
            else:
                g, k = ((base + 4) >> 3) + step // 8, step % 8
            edge = roll(rows(edges[i], g, start_row), 127 - 16 * k)
            left = jnp.where(first_lane, edge, roll(value, 1))
            right = jnp.where(last_lane, edge, roll(value, 127))
            return (left + right) + (value + value)

        return line

    def sweep_planes(line, count, first_row, blocks, first, last, emit, unroll=8, align=0):
        starts = [first_row + 8 * b for b in range(blocks)]
        each = [(i, r) for i in range(count) for r in starts]
        before = [line(i, first - 1, 0, r) for i, r in each]
        current = [line(i, first, 0, r) for i, r in each]
        pair = [a + b for a, b in zip(before, current)]

        def some(base, steps, carry):
            pair, current = carry
            for u in range(steps):
                following = [line(i, base, u + 1, r) for i, r in each]
                later = [a + b for a, b in zip(current, following)]
                sums = [a + b for a, b in zip(pair, later)]
                for b, r in enumerate(starts):
                    emit(base + u, r, [sums[i * blocks + b] for i in range(count)])
                pair, current = later, following
            return tuple(pair), tuple(current)

        head = -(first + align) % unroll if align else 0
        carry = some(first, head, (tuple(pair), tuple(current)))
        start_plane = first + head
        turns = (last - start_plane) // unroll
        if turns > 1:
            carry = lax.fori_loop(0, turns, lambda t, carry: some(start_plane + unroll * t, unroll, carry), carry)
        elif turns == 1:
            carry = some(start_plane, unroll, carry)
        rest = start_plane + turns * unroll
        some(rest, last - rest, carry)

    def slab_pass(edges, emit):
        for b in range(5):
            r = 4 + 8 * b
            sums = []
            for ref in edges:
                parts = [zsum(rows(ref, g, r)) for g in range(6)]
                up = [roll(p, 16) for p in parts]
                down = [roll(p, 112) for p in parts]
                sums.append([
                    (jnp.where(lane < 16, up[max(g - 1, 0)], up[g])
                     + jnp.where(lane >= 112, down[min(g + 1, 5)], down[g]))
                    + (parts[g] + parts[g])
                    for g in range(6)
                ])
            for g in range(6):
                emit(g, r, [s[g] for s in sums])

    def slab_ysum(ref, result, edge):
        for g in range(6):
            for b in range(5):
                value = ysum(ref, g, 4 + 8 * b)
                result[g, pl.ds(4 + 8 * b, 8), :] = value
                edge[g, pl.ds(4 + 8 * b, 8), :] = jnp.where(group == 1, roll(value, 126), roll(value, 116))

    def factors_emit(c, k, q):
        def emit(plane, r, sums):
            at = (plane, pl.ds(r, 8), slice(None))
            centre = c[at]
            k[at] = 64.0 * centre + sums[0]
            q[at] = jnp.where(centre > 0.0, 1.0 / (48.0 * centre + sums[0]), 0.0)

        return emit

    def image_at(at, c, k, u, sums):
        return u[at] * k[at] - (c[at] * sums[0] + sums[1])

    def sweep_emit(c, f, k, q, u, tau, f_scale, u_out, w_out):
        def emit(plane, r, sums):
            at = (plane, pl.ds(r, 8), slice(None))
            rhs = f[at] if f_scale == 1.0 else f_scale * f[at]
            value = u[at] + (tau * q[at]) * (rhs - image_at(at, c, k, u, sums))
            u_out[at] = value
            if w_out is not None:
                w_out[at] = c[at] * value

        return emit

    def residual_emit(c, f, k, u, f_scale, low_plane, low_row, result):
        held = {}

        def emit(plane, r, sums):
            at = (plane, pl.ds(r, 8), slice(None))
            rhs = f[at] if f_scale == 1.0 else f_scale * f[at]
            value = rhs - image_at(at, c, k, u, sums)
            if r not in held:
                held[r] = value
            else:
                result[(plane - low_plane) >> 1, pl.ds(r - low_row, 8), :] = halved(held.pop(r) + value)

        return emit

    row = lax.broadcasted_iota(jnp.int32, (8, 128), 0)

    def build_slab(ref, own, left, right, slab):
        def join(low, middle, high):
            return jnp.where(group < 4, roll(low, 120), jnp.where(group < 12, middle, roll(high, 8)))

        def ends(ref, plane):
            return jnp.where(row < 4, rows(ref, plane, 4), rows(ref, plane, 36))

        def pack(load, first, ks):
            total = jnp.zeros((8, 128), F32)
            for k in ks:
                value = load(first + k)
                total = jnp.where((lane >> 2) == 4 * k + 1, roll(value, 16 * k + 4), total)
                total = jnp.where((lane >> 2) == 4 * k + 2, roll(value, (16 * k + 12) % 128), total)
            return total

        def put(g, first, ks, inner):
            for r in range(8, 40, 8):
                middle = rows(own, g, r) if inner else pack(lambda plane: rows(ref, plane, r), first, ks)
                slab[g, pl.ds(r, 8), :] = join(rows(left, g, r), middle, rows(right, g, r))
            outer = join(ends(left, g), pack(lambda plane: ends(ref, plane), first, ks), ends(right, g))
            slab[g, pl.ds(4, 4), :] = outer[0:4]
            slab[g, pl.ds(40, 4), :] = outer[4:8]

        put(0, -4, range(4, 8), False)
        for g in range(1, 5):
            put(g, 8 * g - 4, range(8), True)
        put(5, 36, range(4), False)

    arrive(msg_c)
    build_slab(c0, oc, ocl, ocr, sc)
    slab_ysum(sc, yc, ec)
    slab_pass([yc], factors_emit(sc, sk, sq))
    sweep_planes(edged([c0], [ec]), 1, 4, 5, 1, 39, factors_emit(c0, k0, q0), U0, 4)

    arrive(msg_f)
    build_slab(f0, of, ofl, ofr, sf)
    scale = 8.0 * tau2[0]
    for g in range(6):
        for b in range(5):
            at = (g, pl.ds(4 + 8 * b, 8), slice(None))
            value = (scale * sq[at]) * sf[at]
            sua[at] = value
            swa[at] = sc[at] * value
    slab_ysum(sua, yu, eu)
    slab_ysum(swa, yw, ew)

    @pl.loop(0, 19)
    def _(i):
        for dx in range(2):
            for b in range(5):
                at = (1 + 2 * i + dx, pl.ds(4 + 8 * b, 8), slice(None))
                value = (scale * q0[at]) * f0[at]
                ua[at] = value
                wa[at] = c0[at] * value

    sweep_planes(edged([ua, wa], [eu, ew]), 2, 4, 5, 2, 38, sweep_emit(c0, f0, k0, q0, ua, tau2[1], 8.0, ub, wb), U0, 4)
    slab_pass([yu, yw], (sweep_emit(sc, sf, sk, sq, sua, tau2[1], 8.0, sub, swb)))
    slab_ysum(sub, yu, eu)
    slab_ysum(swb, yw, ew)
    sweep_planes(edged([ub, wb], [eu, ew]), 2, ROW, 4, 4, 36, residual_emit(c0, f0, k0, ub, 8.0, PX0, ROW, t0), U0, 4)

    @pl.loop(0, 2)
    def _(turn):
        for step in range(8):
            i = 8 * turn + step
            for b in range(2):
                total = t0[i, pl.ds(16 * b, 8, stride=2), :] + t0[i, pl.ds(16 * b + 1, 8, stride=2), :]
                f1[PX1 + i, pl.ds(ROW + 8 * b, 8), :] = jnp.where(own1, 0.5 * pick(total, down1), 0.0)

    pack_coarse(f1, of1, 16, LANE1)
    start(msg_f1)

    sent(msg_c, msg_f, msg_c1, msg_c2)
    def merge(own, left, right, size, width, starts, low, put):
        lanes = size * 4
        at_left = jnp.logical_and(lane >= low - 8, lane < low)
        at_right = jnp.logical_and(lane >= low + lanes, lane < low + lanes + 8)

        def planes(g, ks):
            for k in ks:
                plane = 8 * g + k - 2
                for r in starts:
                    value = jnp.where(at_left, roll(rows(left, g, r), (low - 16 - 16 * k) % 128), rows(own, plane, r))
                    put(plane, r, jnp.where(at_right, roll(rows(right, g, r), (low + lanes - 16 * k) % 128), value))

        planes(0, range(8 - width, 8))
        for g in range(1, 1 + size // 8):
            planes(g, range(8))
        planes(1 + size // 8, range(width))

    def keep(result):
        def put(plane, r, value):
            result[plane, pl.ds(r, 8), :] = value

        return put

    def first_sweep(c, f, q, u, w, tau):
        def put(plane, r, value):
            at = (plane, pl.ds(r, 8), slice(None))
            f[at] = value
            value = (tau * q[at]) * value
            u[at] = value
            w[at] = c[at] * value

        return put

    arrive(msg_c1, msg_c2)
    merge(c1, ocl1, ocr1, 16, W_C1, range(0, 32, 8), LANE1, keep(cm1))
    merge(c2, ocl2, ocr2, 8, W_C2, range(2, 26, 8), LANE2, keep(cm2))
    sweep_planes(plain([cm1]), 1, 4, 3, 2, 26, factors_emit(cm1, k1, q1))
    sweep_planes(plain([cm2]), 1, 3, 3, 1, 19, factors_emit(cm2, k2, q2))

    arrive(msg_f1)
    merge(f1, ofl1, ofr1, 16, W_F1, range(4, 28, 8), LANE1, first_sweep(cm1, fm1, q1, ua1, wa1, tau2[0]))
    sweep_planes(plain([ua1, wa1]), 2, 4, 3, 3, 25, sweep_emit(cm1, fm1, k1, q1, ua1, tau2[1], 1.0, ub1, wb1), U1)
    sweep_planes(plain([ub1, wb1]), 2, ROW, 2, 6, 22, residual_emit(cm1, fm1, k1, ub1, 1.0, PX1, ROW, t1), U1)

    @pl.loop(0, 1)
    def _(turn):
        for step in range(8):
            i = 8 * turn + step
            total = t1[i, pl.ds(0, 8, stride=2), :] + t1[i, pl.ds(1, 8, stride=2), :]
            f2[PX1 + i, pl.ds(ROW, 8), :] = jnp.where(own2, 0.5 * pick(total, down2), 0.0)

    pack_coarse(f2, of2, 8, LANE2)
    start(msg_f2)

    sent(msg_f1)
    arrive(msg_f2)
    merge(f2, ofl2, ofr2, 8, W_F2, range(3, 27, 8), LANE2, first_sweep(cm2, fm2, q2, ua2, wa2, tau4[0]))
    sweep_planes(plain([ua2, wa2]), 2, 4, 2, 2, 18, sweep_emit(cm2, fm2, k2, q2, ua2, tau4[1], 1.0, ub2, wb2), U2)
    sweep_planes(plain([ub2, wb2]), 2, 4, 2, 3, 17, sweep_emit(cm2, fm2, k2, q2, ub2, tau4[2], 1.0, ua2, wa2), U2)
    sweep_planes(plain([ua2, wa2]), 2, 4, 2, 4, 16, sweep_emit(cm2, fm2, k2, q2, ua2, tau4[3], 1.0, ub2, None), U2)

    sent(msg_f2)

    up = 32 + (lane >> 1)

    @pl.loop(0, 2)
    def _(turn):
        for step in range(6):
            i = 6 * turn + step
            for b in range(2):
                value = pick(rows(ub2, 4 + i, 6 + 8 * b), up)
                p1s[i, pl.ds(16 * b, 8, stride=2), :] = value
                p1s[i, pl.ds(16 * b + 1, 8, stride=2), :] = value

    @pl.loop(0, 4)
    def _(turn):
        for step in range(3):
            i = 3 * turn + step
            for dx in range(2):
                for b in range(3):
                    at = (2 + 2 * i + dx, pl.ds(4 + 8 * b, 8), slice(None))
                    value = ub1[at] + p1s[i, pl.ds(8 * b, 8), :]
                    ua1[at] = value
                    wa1[at] = cm1[at] * value

    sweep_planes(plain([ua1, wa1]), 2, 4, 3, 4, 24, sweep_emit(cm1, fm1, k1, q1, ua1, tau2[0], 1.0, ub1, wb1), U1)
    sweep_planes(plain([ub1, wb1]), 2, 4, 3, 5, 23, sweep_emit(cm1, fm1, k1, q1, ub1, tau2[1], 1.0, ua1, None), U1)

    side = 32 + ((group - 4 + jnp.where(group >= 8, 120, 0)) >> 1)

    @pl.loop(0, 3)
    def _(turn):
        for step in range(6):
            i = 6 * turn + step
            for b in range(3):
                value = pick(rows(ua1, 5 + i, 6 + 8 * b), up)
                p0s[i, pl.ds(16 * b, 8, stride=2), :] = value
                p0s[i, pl.ds(16 * b + 1, 8, stride=2), :] = value

    @pl.loop(0, 18)
    def _(i):
        for dx in range(2):
            for b in range(5):
                at = (2 + 2 * i + dx, pl.ds(4 + 8 * b, 8), slice(None))
                value = ub[at] + p0s[i, pl.ds(8 * b, 8), :]
                ua[at] = value
                wa[at] = c0[at] * value

    @pl.loop(0, 6)
    def _(g):
        for b in range(3):
            total = jnp.zeros((8, 128), F32)
            for m in range(4):
                total = jnp.where((lane >> 5) == m, pick(rows(ua1, 4 * g + 2 + m, 6 + 8 * b), side), total)
            sp[g, pl.ds(16 * b, 8, stride=2), :] = total
            sp[g, pl.ds(16 * b + 1, 8, stride=2), :] = total
        for b in range(5):
            at = (g, pl.ds(4 + 8 * b, 8), slice(None))
            value = sub[at] + sp[g, pl.ds(8 * b, 8), :]
            sua[at] = value
            swa[at] = sc[at] * value

    slab_ysum(sua, yu, eu)
    slab_ysum(swa, yw, ew)
    sweep_planes(edged([ua, wa], [eu, ew]), 2, 4, 5, 3, 37, sweep_emit(c0, f0, k0, q0, ua, tau2[0], 8.0, ub, wb), U0, 4)
    slab_pass([yu, yw], (sweep_emit(sc, sf, sk, sq, sua, tau2[0], 8.0, sub, swb)))
    slab_ysum(sub, yu, eu)
    slab_ysum(swb, yw, ew)

    def last_emit(plane, r, sums):
        at = (plane, pl.ds(r, 8), slice(None))
        value = ub[at] + (tau2[1] * q0[at]) * (8.0 * f0[at] - image_at(at, c0, k0, ub, sums))
        out_ref[plane - PX0, pl.ds(r - ROW, 8), :] = value

    sweep_planes(edged([ub, wb], [eu, ew]), 2, ROW, 4, 4, 36, last_emit, U0, 4)


def solution(mesh):
    shape = tuple(mesh.shape[a] for a in ("gx", "gy", "gz"))
    count = 26 * 6
    big = [pltpu.VMEM((40, 48, 128), F32)] * 8
    slabs = [pltpu.VMEM((6, 48, 128), F32)] * 21
    level1 = [pltpu.VMEM((28, 32, 128), F32)] * 10 + [pltpu.VMEM((4, 32, 128), F32)] * 6
    level2 = [pltpu.VMEM((20, 32, 128), F32)] * 10 + [pltpu.VMEM((3, 32, 128), F32)] * 6
    between = [
        pltpu.VMEM((16, 32, 128), F32), pltpu.VMEM((18, 48, 128), F32),
        pltpu.VMEM((8, 16, 128), F32), pltpu.VMEM((12, 32, 128), F32),
    ]

    def per_device(right_side, coefficient):
        return pl.pallas_call(
            functools.partial(kernel, shape),
            out_shape=jax.ShapeDtypeStruct(right_side.shape, F32),
            in_specs=[pl.BlockSpec(memory_space=pl.ANY)] * 2,
            out_specs=pl.BlockSpec(memory_space=pltpu.VMEM),
            scratch_shapes=big + slabs + between + level1 + level2 + [
                pltpu.SemaphoreType.DMA((2,)),
                pltpu.SemaphoreType.DMA((count,)),
                pltpu.SemaphoreType.DMA((count,)),
            ],
            compiler_params=pltpu.CompilerParams(
                collective_id=0, has_side_effects=True, vmem_limit_bytes=24 * 1024 * 1024
            ),
        )(*(pltpu.with_memory_space_constraint(x, pltpu.HBM) for x in (right_side, coefficient)))

    placed = P("gx", "gy", "gz")
    return jax.shard_map(per_device, mesh=mesh, in_specs=(placed, placed), out_specs=placed, check_vma=False)
```

```python
import functools
import math

import jax
import jax.numpy as jnp
from jax import lax
from jax.experimental import pallas as pl
from jax.experimental.pallas import tpu as pltpu
from jax.sharding import PartitionSpec as P

MESH = pl.DeviceIdType.MESH
F32 = jnp.float32

PX0, ROW = 4, 8
PX1 = 6
U0, U1, U2 = 16, 12, 16
W_C0, W_F0, W_C1, W_C2, W_F1, W_F2 = 4, 3, 5, 6, 4, 5
LANE1, LANE2 = 32, 48

DIRS = [(a, b, c) for a in (-1, 0, 1) for b in (-1, 0, 1) for c in (-1, 0, 1) if (a, b, c) != (0, 0, 0)]
FLAT = [d for d in DIRS if d[2] == 0]
DEEP = [d for d in DIRS if d[2] != 0]


def step_sizes(sweeps):
    return [1.0 / (1.15 + 0.85 * math.cos(math.pi * (2 * j + 1) / (2 * sweeps))) for j in range(sweeps)]


def cut(step, low, size, width):
    if step == 0:
        return pl.ds(low, size), pl.ds(low, size)
    if step > 0:
        return pl.ds(low + size - width, width), pl.ds(low - width, width)
    return pl.ds(low, width), pl.ds(low + size, width)


def kernel(
    shape, right_hbm, coef_hbm, out_ref,
    c0, f0, k0, q0, ua, wa, ub, wb,
    oc, ocl, ocr, of, ofl, ofr,
    sc, sf, sk, sq, sua, swa, sub, swb, yc, yu, yw, ec, eu, ew, sp,
    t0, p0s, t1, p1s,
    c1, f1, cm1, fm1, k1, q1, ua1, wa1, ub1, wb1,
    oc1, ocl1, ocr1, of1, ofl1, ofr1,
    c2, f2, cm2, fm2, k2, q2, ua2, wa2, ub2, wb2,
    oc2, ocl2, ocr2, of2, ofl2, ofr2,
    in_sem, send_sem, recv_sem,
):
    spot = [lax.axis_index(a) for a in ("gx", "gy", "gz")]
    below = [s > 0 for s in spot]
    above = [s < n - 1 for s, n in zip(spot, shape)]

    def exists(d):
        found = None
        for axis, step in enumerate(d):
            if step != 0:
                one = above[axis] if step > 0 else below[axis]
                found = one if found is None else jnp.logical_and(found, one)
        return found

    def opposite(d):
        return tuple(-s for s in d)

    def device(d):
        return tuple(s + step for s, step in zip(spot, d))

    lane = lax.broadcasted_iota(jnp.int32, (8, 128), 1)
    group = lane & 15
    tau2 = step_sizes(2)
    tau4 = step_sizes(4)

    def roll(value, shift):
        return pltpu.roll(value, shift, axis=1)

    def pick(value, index):
        return jnp.take_along_axis(value, index, axis=1, mode="promise_in_bounds")

    def rows(ref, plane, start):
        return ref[plane, pl.ds(start, 8), :]

    in_c = pltpu.make_async_copy(coef_hbm, c0.at[pl.ds(PX0, 32), pl.ds(ROW, 32)], in_sem.at[0])
    in_f = pltpu.make_async_copy(right_hbm, f0.at[pl.ds(PX0, 32), pl.ds(ROW, 32)], in_sem.at[1])
    in_c.start()
    in_f.start()

    far_first = sorted(DIRS, key=lambda d: -sum(abs(s) for s in d))

    barrier = pltpu.get_barrier_semaphore()
    for d in far_first:
        @pl.when(exists(d))
        def _():
            pl.semaphore_signal(barrier, inc=1, device_id=device(d), device_id_type=MESH)

    zero = jnp.zeros((8, 128), F32)
    flat = [(c0, PX0, 32, 32), (f0, PX0, 32, 32), (c1, PX1, 16, 16), (f1, PX1, 16, 16), (c2, PX1, 8, 8), (f2, PX1, 8, 8)]
    lefts = [(ocl, 1, 4, 32), (ofl, 1, 4, 32), (ocl1, 1, 2, 16), (ofl1, 1, 2, 16), (ocl2, 1, 1, 8), (ofl2, 1, 1, 8)]
    rights = [(ocr, 1, 4, 32), (ofr, 1, 4, 32), (ocr1, 1, 2, 16), (ofr1, 1, 2, 16), (ocr2, 1, 1, 8), (ofr2, 1, 1, 8)]

    def clear(ref, first, last, starts):
        @pl.loop(first, last)
        def _(i):
            for r in starts:
                ref[i, pl.ds(r, 8), :] = zero

    for axis in range(3):
        for side, present in ((0, below[axis]), (1, above[axis])):
            @pl.when(jnp.logical_not(present))
            def _():
                if axis == 2:
                    for ref, low, size_x, size_y in (lefts, rights)[side]:
                        clear(ref, 0, 2 * low + size_x, range(0, size_y + 16, 8))
                else:
                    for ref, low, size_x, size_y in flat + lefts + rights:
                        if axis == 0:
                            first = (0, low + size_x)[side]
                            clear(ref, first, first + low, range(0, size_y + 16, 8))
                        else:
                            clear(ref, 0, 2 * low + size_x, [(0, 8 + size_y)[side]])

    counter = [0]

    def message(d, src, dst):
        slot = counter[0]
        counter[0] += 1
        return pltpu.make_async_remote_copy(
            src_ref=src, dst_ref=dst, send_sem=send_sem.at[slot], recv_sem=recv_sem.at[slot],
            device_id=device(d), device_id_type=MESH,
        )

    def flat_messages(own, low, size, width):
        found = {}
        for d in FLAT:
            from_x, to_x = cut(d[0], low, size, width)
            from_y, to_y = cut(d[1], ROW, size, width)
            found[d] = [message(d, own.at[from_x, from_y], own.at[to_x, to_y])]
        return found

    def slab_messages(own, left, right, size, width):
        found = {}
        for d in DEEP:
            from_x, to_x = cut(d[0], 1, size // 8, 1)
            from_y, to_y = cut(d[1], ROW, size, width)
            target = left if d[2] > 0 else right
            found[d] = [message(d, own.at[from_x, from_y], target.at[to_x, to_y])]
        return found

    def messages(own, low, slab, left, right, size, width):
        return {**flat_messages(own, low, size, width), **slab_messages(slab, left, right, size, width)}

    msg_c = messages(c0, PX0, oc, ocl, ocr, 32, W_C0)
    msg_f = messages(f0, PX0, of, ofl, ofr, 32, W_F0)
    msg_c1 = messages(c1, PX1, oc1, ocl1, ocr1, 16, W_C1)
    msg_c2 = messages(c2, PX1, oc2, ocl2, ocr2, 8, W_C2)
    msg_f1 = messages(f1, PX1, of1, ofl1, ofr1, 16, W_F1)
    msg_f2 = messages(f2, PX1, of2, ofl2, ofr2, 8, W_F2)


    def start(*groups):
        for d in far_first:
            @pl.when(exists(d))
            def _():
                for found in groups:
                    for copy in found[d]:
                        copy.start()

    def arrive(*groups):
        for d in DIRS:
            @pl.when(exists(opposite(d)))
            def _():
                for found in groups:
                    for copy in found[d]:
                        copy.wait_recv()

    def sent(*groups):
        for d in DIRS:
            @pl.when(exists(d))
            def _():
                for found in groups:
                    for copy in found[d]:
                        copy.wait_send()

    def packed(ref, first, ks, start_row):
        total = jnp.zeros((8, 128), F32)
        for k in ks:
            value = rows(ref, first + k, start_row)
            low = roll(value, 16 * k + 4)
            high = roll(value, (16 * k + 12) % 128)
            total = jnp.where((lane >> 2) == 4 * k + 1, low, total)
            total = jnp.where((lane >> 2) == 4 * k + 2, high, total)
        return total

    def pack_own(ref, slab):
        for g in range(4):
            for b in range(4):
                slab[1 + g, pl.ds(ROW + 8 * b, 8), :] = packed(ref, PX0 + 8 * g, range(8), ROW + 8 * b)

    def pack_coarse(ref, slab, size, low):
        width = size * 4
        for g in range(size // 8):
            for b in range(size // 8):
                total = jnp.zeros((8, 128), F32)
                for k in range(8):
                    value = rows(ref, PX1 + 8 * g + k, ROW + 8 * b)
                    total = jnp.where((lane >> 3) == 2 * k, roll(value, (16 * k - low) % 128), total)
                    total = jnp.where((lane >> 3) == 2 * k + 1, roll(value, (16 * k + 16 - low - width) % 128), total)
                slab[1 + g, pl.ds(ROW + 8 * b, 8), :] = total

    in_c.wait()
    pack_own(c0, oc)
    in_f.wait()
    pack_own(f0, of)
    pl.semaphore_wait(
        barrier,
        math.prod(1 + b.astype(jnp.int32) + a.astype(jnp.int32) for b, a in zip(below, above)) - 1,
    )
    start(msg_c)
    start(msg_f)

    def halved(value):
        return value + roll(value, 127)

    down1 = jnp.clip(2 * (lane - LANE1), 0, 127)
    own1 = jnp.logical_and(lane >= LANE1, lane < LANE1 + 64)
    down2 = jnp.clip(LANE1 + 2 * (lane - LANE2), 0, 127)
    own2 = jnp.logical_and(lane >= LANE2, lane < LANE2 + 32)

    @pl.loop(0, 4)
    def _(turn):
        for step in range(4):
            i = 4 * turn + step
            for b in range(2):
                total = None
                for dx in range(2):
                    for dy in range(2):
                        part = c0[PX0 + 2 * i + dx, pl.ds(ROW + 16 * b + dy, 8, stride=2), :]
                        total = part if total is None else total + part
                c1[PX1 + i, pl.ds(ROW + 8 * b, 8), :] = jnp.where(own1, 0.125 * pick(halved(total), down1), 0.0)

    @pl.loop(0, 2)
    def _(turn):
        for step in range(4):
            i = 4 * turn + step
            total = None
            for dx in range(2):
                for dy in range(2):
                    part = c1[PX1 + 2 * i + dx, pl.ds(ROW + dy, 8, stride=2), :]
                    total = part if total is None else total + part
            c2[PX1 + i, pl.ds(ROW, 8), :] = jnp.where(own2, 0.125 * pick(halved(total), down2), 0.0)

    pack_coarse(c1, oc1, 16, LANE1)
    pack_coarse(c2, oc2, 8, LANE2)
    start(msg_c1, msg_c2)

    def ysum(ref, plane, start_row):
        above_, here, below_ = (rows(ref, plane, start_row + s) for s in (-1, 0, 1))
        return (above_ + below_) + (here + here)

    def zsum(value):
        return (roll(value, 1) + roll(value, 127)) + (value + value)

    def plain(refs):
        def line(i, base, step, start_row):
            return zsum(ysum(refs[i], base + step, start_row))

        return line

    first_lane, last_lane = lane == 0, lane == 127

    def edged(refs, edges):
        def line(i, base, step, start_row):
            value = ysum(refs[i], base + step, start_row)
            if isinstance(base, int):
                g, k = divmod(base + step + 4, 8)
            else:
                g, k = ((base + 4) >> 3) + step // 8, step % 8
            edge = roll(rows(edges[i], g, start_row), 127 - 16 * k)
            left = jnp.where(first_lane, edge, roll(value, 1))
            right = jnp.where(last_lane, edge, roll(value, 127))
            return (left + right) + (value + value)

        return line

    def sweep_planes(line, count, first_row, blocks, first, last, emit, unroll=8, align=0):
        starts = [first_row + 8 * b for b in range(blocks)]
        each = [(i, r) for i in range(count) for r in starts]
        before = [line(i, first - 1, 0, r) for i, r in each]
        current = [line(i, first, 0, r) for i, r in each]
        pair = [a + b for a, b in zip(before, current)]

        def some(base, steps, carry):
            pair, current = carry
            for u in range(steps):
                following = [line(i, base, u + 1, r) for i, r in each]
                later = [a + b for a, b in zip(current, following)]
                sums = [a + b for a, b in zip(pair, later)]
                for b, r in enumerate(starts):
                    emit(base + u, r, [sums[i * blocks + b] for i in range(count)])
                pair, current = later, following
            return tuple(pair), tuple(current)

        head = -(first + align) % unroll if align else 0
        carry = some(first, head, (tuple(pair), tuple(current)))
        start_plane = first + head
        turns = (last - start_plane) // unroll
        if turns > 1:
            carry = lax.fori_loop(0, turns, lambda t, carry: some(start_plane + unroll * t, unroll, carry), carry)
        elif turns == 1:
            carry = some(start_plane, unroll, carry)
        rest = start_plane + turns * unroll
        some(rest, last - rest, carry)

    def slab_pass(edges, emit):
        for b in range(5):
            r = 4 + 8 * b
            sums = []
            for ref in edges:
                parts = [zsum(rows(ref, g, r)) for g in range(6)]
                up = [roll(p, 16) for p in parts]
                down = [roll(p, 112) for p in parts]
                sums.append([
                    (jnp.where(lane < 16, up[max(g - 1, 0)], up[g])
                     + jnp.where(lane >= 112, down[min(g + 1, 5)], down[g]))
                    + (parts[g] + parts[g])
                    for g in range(6)
                ])
            for g in range(6):
                emit(g, r, [s[g] for s in sums])

    def slab_ysum(ref, result, edge):
        for g in range(6):
            for b in range(5):
                value = ysum(ref, g, 4 + 8 * b)
                result[g, pl.ds(4 + 8 * b, 8), :] = value
                edge[g, pl.ds(4 + 8 * b, 8), :] = jnp.where(group == 1, roll(value, 126), roll(value, 116))

    def factors_emit(c, k, q):
        def emit(plane, r, sums):
            at = (plane, pl.ds(r, 8), slice(None))
            centre = c[at]
            k[at] = 64.0 * centre + sums[0]
            q[at] = jnp.where(centre > 0.0, 1.0 / (48.0 * centre + sums[0]), 0.0)

        return emit

    def image_at(at, c, k, u, sums):
        return u[at] * k[at] - (c[at] * sums[0] + sums[1])

    def sweep_emit(c, f, k, q, u, tau, f_scale, u_out, w_out):
        def emit(plane, r, sums):
            at = (plane, pl.ds(r, 8), slice(None))
            rhs = f[at] if f_scale == 1.0 else f_scale * f[at]
            value = u[at] + (tau * q[at]) * (rhs - image_at(at, c, k, u, sums))
            u_out[at] = value
            if w_out is not None:
                w_out[at] = c[at] * value

        return emit

    def residual_emit(c, f, k, u, f_scale, low_plane, low_row, result):
        held = {}

        def emit(plane, r, sums):
            at = (plane, pl.ds(r, 8), slice(None))
            rhs = f[at] if f_scale == 1.0 else f_scale * f[at]
            value = rhs - image_at(at, c, k, u, sums)
            if r not in held:
                held[r] = value
            else:
                result[(plane - low_plane) >> 1, pl.ds(r - low_row, 8), :] = halved(held.pop(r) + value)

        return emit

    row = lax.broadcasted_iota(jnp.int32, (8, 128), 0)

    def build_slab(ref, own, left, right, slab):
        def join(low, middle, high):
            return jnp.where(group < 4, roll(low, 120), jnp.where(group < 12, middle, roll(high, 8)))

        def ends(ref, plane):
            return jnp.where(row < 4, rows(ref, plane, 4), rows(ref, plane, 36))

        def pack(load, first, ks):
            total = jnp.zeros((8, 128), F32)
            for k in ks:
                value = load(first + k)
                total = jnp.where((lane >> 2) == 4 * k + 1, roll(value, 16 * k + 4), total)
                total = jnp.where((lane >> 2) == 4 * k + 2, roll(value, (16 * k + 12) % 128), total)
            return total

        def put(g, first, ks, inner):
            for r in range(8, 40, 8):
                middle = rows(own, g, r) if inner else pack(lambda plane: rows(ref, plane, r), first, ks)
                slab[g, pl.ds(r, 8), :] = join(rows(left, g, r), middle, rows(right, g, r))
            outer = join(ends(left, g), pack(lambda plane: ends(ref, plane), first, ks), ends(right, g))
            slab[g, pl.ds(4, 4), :] = outer[0:4]
            slab[g, pl.ds(40, 4), :] = outer[4:8]

        put(0, -4, range(4, 8), False)
        for g in range(1, 5):
            put(g, 8 * g - 4, range(8), True)
        put(5, 36, range(4), False)

    arrive(msg_c)
    build_slab(c0, oc, ocl, ocr, sc)
    slab_ysum(sc, yc, ec)
    slab_pass([yc], factors_emit(sc, sk, sq))
    sweep_planes(edged([c0], [ec]), 1, 4, 5, 1, 39, factors_emit(c0, k0, q0), U0, 4)

    arrive(msg_f)
    build_slab(f0, of, ofl, ofr, sf)
    scale = 8.0 * tau2[0]
    for g in range(6):
        for b in range(5):
            at = (g, pl.ds(4 + 8 * b, 8), slice(None))
            value = (scale * sq[at]) * sf[at]
            sua[at] = value
            swa[at] = sc[at] * value
    slab_ysum(sua, yu, eu)
    slab_ysum(swa, yw, ew)

    @pl.loop(0, 19)
    def _(i):
        for dx in range(2):
            for b in range(5):
                at = (1 + 2 * i + dx, pl.ds(4 + 8 * b, 8), slice(None))
                value = (scale * q0[at]) * f0[at]
                ua[at] = value
                wa[at] = c0[at] * value

    sweep_planes(edged([ua, wa], [eu, ew]), 2, 4, 5, 2, 38, sweep_emit(c0, f0, k0, q0, ua, tau2[1], 8.0, ub, wb), U0, 4)
    slab_pass([yu, yw], (sweep_emit(sc, sf, sk, sq, sua, tau2[1], 8.0, sub, swb)))
    slab_ysum(sub, yu, eu)
    slab_ysum(swb, yw, ew)
    sweep_planes(edged([ub, wb], [eu, ew]), 2, ROW, 4, 4, 36, residual_emit(c0, f0, k0, ub, 8.0, PX0, ROW, t0), U0, 4)

    for i in range(16):
        for b in range(2):
            total = t0[i, pl.ds(16 * b, 8, stride=2), :] + t0[i, pl.ds(16 * b + 1, 8, stride=2), :]
            f1[PX1 + i, pl.ds(ROW + 8 * b, 8), :] = jnp.where(own1, 0.5 * pick(total, down1), 0.0)

    pack_coarse(f1, of1, 16, LANE1)
    start(msg_f1)

    sent(msg_c, msg_f, msg_c1, msg_c2)
    def merge(own, left, right, size, width, starts, low, put):
        lanes = size * 4
        at_left = jnp.logical_and(lane >= low - 8, lane < low)
        at_right = jnp.logical_and(lane >= low + lanes, lane < low + lanes + 8)

        def planes(g, ks):
            for k in ks:
                plane = 8 * g + k - 2
                for r in starts:
                    value = jnp.where(at_left, roll(rows(left, g, r), (low - 16 - 16 * k) % 128), rows(own, plane, r))
                    put(plane, r, jnp.where(at_right, roll(rows(right, g, r), (low + lanes - 16 * k) % 128), value))

        planes(0, range(8 - width, 8))
        for g in range(1, 1 + size // 8):
            planes(g, range(8))
        planes(1 + size // 8, range(width))

    def keep(result):
        def put(plane, r, value):
            result[plane, pl.ds(r, 8), :] = value

        return put

    def first_sweep(c, f, q, u, w, tau):
        def put(plane, r, value):
            at = (plane, pl.ds(r, 8), slice(None))
            f[at] = value
            value = (tau * q[at]) * value
            u[at] = value
            w[at] = c[at] * value

        return put

    arrive(msg_c1, msg_c2)
    merge(c1, ocl1, ocr1, 16, W_C1, range(0, 32, 8), LANE1, keep(cm1))
    merge(c2, ocl2, ocr2, 8, W_C2, range(2, 26, 8), LANE2, keep(cm2))
    sweep_planes(plain([cm1]), 1, 4, 3, 2, 26, factors_emit(cm1, k1, q1))
    sweep_planes(plain([cm2]), 1, 3, 3, 1, 19, factors_emit(cm2, k2, q2))

    arrive(msg_f1)
    merge(f1, ofl1, ofr1, 16, W_F1, range(4, 28, 8), LANE1, first_sweep(cm1, fm1, q1, ua1, wa1, tau2[0]))
    sweep_planes(plain([ua1, wa1]), 2, 4, 3, 3, 25, sweep_emit(cm1, fm1, k1, q1, ua1, tau2[1], 1.0, ub1, wb1), U1)
    sweep_planes(plain([ub1, wb1]), 2, ROW, 2, 6, 22, residual_emit(cm1, fm1, k1, ub1, 1.0, PX1, ROW, t1), U1)

    for i in range(8):
        total = t1[i, pl.ds(0, 8, stride=2), :] + t1[i, pl.ds(1, 8, stride=2), :]
        f2[PX1 + i, pl.ds(ROW, 8), :] = jnp.where(own2, 0.5 * pick(total, down2), 0.0)

    pack_coarse(f2, of2, 8, LANE2)
    start(msg_f2)

    sent(msg_f1)
    arrive(msg_f2)
    merge(f2, ofl2, ofr2, 8, W_F2, range(3, 27, 8), LANE2, first_sweep(cm2, fm2, q2, ua2, wa2, tau4[0]))
    sweep_planes(plain([ua2, wa2]), 2, 4, 2, 2, 18, sweep_emit(cm2, fm2, k2, q2, ua2, tau4[1], 1.0, ub2, wb2), U2)
    sweep_planes(plain([ub2, wb2]), 2, 4, 2, 3, 17, sweep_emit(cm2, fm2, k2, q2, ub2, tau4[2], 1.0, ua2, wa2), U2)
    sweep_planes(plain([ua2, wa2]), 2, 4, 2, 4, 16, sweep_emit(cm2, fm2, k2, q2, ua2, tau4[3], 1.0, ub2, None), U2)

    sent(msg_f2)

    up = 32 + (lane >> 1)

    for i in range(12):
        for b in range(2):
            value = pick(rows(ub2, 4 + i, 6 + 8 * b), up)
            p1s[i, pl.ds(16 * b, 8, stride=2), :] = value
            p1s[i, pl.ds(16 * b + 1, 8, stride=2), :] = value

    @pl.loop(0, 4)
    def _(turn):
        for step in range(3):
            i = 3 * turn + step
            for dx in range(2):
                for b in range(3):
                    at = (2 + 2 * i + dx, pl.ds(4 + 8 * b, 8), slice(None))
                    value = ub1[at] + p1s[i, pl.ds(8 * b, 8), :]
                    ua1[at] = value
                    wa1[at] = cm1[at] * value

    sweep_planes(plain([ua1, wa1]), 2, 4, 3, 4, 24, sweep_emit(cm1, fm1, k1, q1, ua1, tau2[0], 1.0, ub1, wb1), U1)
    sweep_planes(plain([ub1, wb1]), 2, 4, 3, 5, 23, sweep_emit(cm1, fm1, k1, q1, ub1, tau2[1], 1.0, ua1, None), U1)

    side = 32 + ((group - 4 + jnp.where(group >= 8, 120, 0)) >> 1)

    for i in range(18):
        for b in range(3):
            value = pick(rows(ua1, 5 + i, 6 + 8 * b), up)
            p0s[i, pl.ds(16 * b, 8, stride=2), :] = value
            p0s[i, pl.ds(16 * b + 1, 8, stride=2), :] = value

    @pl.loop(0, 18)
    def _(i):
        for dx in range(2):
            for b in range(5):
                at = (2 + 2 * i + dx, pl.ds(4 + 8 * b, 8), slice(None))
                value = ub[at] + p0s[i, pl.ds(8 * b, 8), :]
                ua[at] = value
                wa[at] = c0[at] * value

    for g in range(6):
        for b in range(3):
            total = jnp.zeros((8, 128), F32)
            for m in range(4):
                total = jnp.where((lane >> 5) == m, pick(rows(ua1, 4 * g + 2 + m, 6 + 8 * b), side), total)
            sp[g, pl.ds(16 * b, 8, stride=2), :] = total
            sp[g, pl.ds(16 * b + 1, 8, stride=2), :] = total
        for b in range(5):
            at = (g, pl.ds(4 + 8 * b, 8), slice(None))
            value = sub[at] + sp[g, pl.ds(8 * b, 8), :]
            sua[at] = value
            swa[at] = sc[at] * value

    slab_ysum(sua, yu, eu)
    slab_ysum(swa, yw, ew)
    sweep_planes(edged([ua, wa], [eu, ew]), 2, 4, 5, 3, 37, sweep_emit(c0, f0, k0, q0, ua, tau2[0], 8.0, ub, wb), U0, 4)
    slab_pass([yu, yw], (sweep_emit(sc, sf, sk, sq, sua, tau2[0], 8.0, sub, swb)))
    slab_ysum(sub, yu, eu)
    slab_ysum(swb, yw, ew)

    def last_emit(plane, r, sums):
        at = (plane, pl.ds(r, 8), slice(None))
        value = ub[at] + (tau2[1] * q0[at]) * (8.0 * f0[at] - image_at(at, c0, k0, ub, sums))
        out_ref[plane - PX0, pl.ds(r - ROW, 8), :] = value

    sweep_planes(edged([ub, wb], [eu, ew]), 2, ROW, 4, 4, 36, last_emit, U0, 4)


def solution(mesh):
    shape = tuple(mesh.shape[a] for a in ("gx", "gy", "gz"))
    count = 26 * 6
    big = [pltpu.VMEM((40, 48, 128), F32)] * 8
    slabs = [pltpu.VMEM((6, 48, 128), F32)] * 21
    level1 = [pltpu.VMEM((28, 32, 128), F32)] * 10 + [pltpu.VMEM((4, 32, 128), F32)] * 6
    level2 = [pltpu.VMEM((20, 32, 128), F32)] * 10 + [pltpu.VMEM((3, 32, 128), F32)] * 6
    between = [
        pltpu.VMEM((16, 32, 128), F32), pltpu.VMEM((18, 48, 128), F32),
        pltpu.VMEM((8, 16, 128), F32), pltpu.VMEM((12, 32, 128), F32),
    ]

    def per_device(right_side, coefficient):
        return pl.pallas_call(
            functools.partial(kernel, shape),
            out_shape=jax.ShapeDtypeStruct(right_side.shape, F32),
            in_specs=[pl.BlockSpec(memory_space=pl.ANY)] * 2,
            out_specs=pl.BlockSpec(memory_space=pltpu.VMEM),
            scratch_shapes=big + slabs + between + level1 + level2 + [
                pltpu.SemaphoreType.DMA((2,)),
                pltpu.SemaphoreType.DMA((count,)),
                pltpu.SemaphoreType.DMA((count,)),
            ],
            compiler_params=pltpu.CompilerParams(
                collective_id=0, has_side_effects=True, vmem_limit_bytes=24 * 1024 * 1024
            ),
        )(*(pltpu.with_memory_space_constraint(x, pltpu.HBM) for x in (right_side, coefficient)))

    placed = P("gx", "gy", "gz")
    return jax.shard_map(per_device, mesh=mesh, in_specs=(placed, placed), out_specs=placed, check_vma=False)
```
